512 devices in a mesh: dp: 16 (over z_lo, core), center: 32 (over x, y, z_hi).
Axes of the slice: x: 4, y: 4, z: 16 (z_hi: 2, z_lo: 8; z = z_hi * 8 + z_lo), core: 2. Of those that a mesh axis runs over, the one named last changes fastest.
Arguments:
- features: bfloat16 [16384, 1024], P('dp'), may hold values from -6 to 6
- centers: bfloat16 [16384, 1024], P('center'), may hold values from -6 to 6
- targets: bfloat16 [16384, 256], P('dp'), may hold values from -6 to 6
Outputs:
- coef: float32 [16384, 256], P('center')
- residual: float32 [16384, 256], P('center')
The draws below stay inside these ranges and needn't reach their ends.
All inputs are finite; a program needn't handle non-finite values.
Results may differ from the reference program's by a relative error of at most 0.024.
Values may be sent and summed in bfloat16 or wider, within the bound.
A program may use at most 64 MiB of HBM per device.

```python
import math
import jax
import jax.numpy as jnp
from jax import lax

D = 1024
TARGETS = 256
N_DEV = 1024
ITERS = 2
EXAMPLES = 16384
CENTERS = 16384


def level_of(stream_key, shape, cuts, low, top_value):
    loudness = 1.0
    for axis_at, blocks in cuts:
        heights = jax.random.uniform(jax.random.fold_in(jax.random.fold_in(stream_key, 6), axis_at), (blocks,), jnp.float32, low / len(cuts), top_value / len(cuts))
        loudness = loudness * jnp.repeat(jnp.exp(heights), shape[axis_at] // blocks).reshape((-1,) + (1,) * (len(shape) - 1 - axis_at))
    return loudness


def noise(rng, extent, width, bound, shards=(), kind=jnp.bfloat16):
    entries = width * jax.random.normal(rng, extent, jnp.float32)
    if shards:
        entries = entries * level_of(rng, extent, shards, -0.22, 0.18)
    return jnp.clip(entries, -bound, bound).astype(kind)


def setup_inputs(seed: int = 0) -> dict:
    arg_keys = jax.random.split(jax.random.key(seed), 4)
    return {
        "features": noise(arg_keys[0], (EXAMPLES, D), 1.0, 6.0, ((0, 16),)),
        "centers": noise(arg_keys[1], (CENTERS, D), 1.0, 6.0, ((0, 32),)),
        "targets": noise(arg_keys[2], (EXAMPLES, TARGETS), 1.0, 6.0, ((0, 16),)),
    }


def kernel_block(rows, centers):
    scores = lax.dot_general(rows, centers, (((1,), (1,)), ((), ())), preferred_element_type=jnp.float32)
    lifted = 1.0 + 0.5 / math.sqrt(rows.shape[1]) * scores
    return (lifted * lifted * lifted).astype(jnp.bfloat16)

def transposed_dot(kernel, values):
    return lax.dot_general(kernel, values, (((0,), (0,)), ((), ())), preferred_element_type=jnp.float32)

def right_hand(features, centers, targets):
    blocks = features.shape[0] // N_DEV

    def one_block(total, block_index):
        rows = lax.dynamic_slice_in_dim(features, block_index * N_DEV, N_DEV, 0)
        values = lax.dynamic_slice_in_dim(targets, block_index * N_DEV, N_DEV, 0)
        kernel = kernel_block(rows, centers)
        return (total + transposed_dot(kernel, values), None)
    start = jnp.zeros((centers.shape[0], targets.shape[1]), jnp.float32)
    total, unused = lax.scan(one_block, start, jnp.arange(blocks, dtype=jnp.int32))
    return total / math.sqrt(features.shape[0])

def apply_operator(features, centers, direction):
    blocks = features.shape[0] // N_DEV
    low_dir = direction.astype(jnp.bfloat16)

    def one_block(total, block_index):
        rows = lax.dynamic_slice_in_dim(features, block_index * N_DEV, N_DEV, 0)
        kernel = kernel_block(rows, centers)
        predicted = jnp.dot(kernel, low_dir, preferred_element_type=jnp.float32).astype(jnp.bfloat16)
        return (total + transposed_dot(kernel, predicted), None)
    start = jnp.zeros(direction.shape, jnp.float32)
    total, unused = lax.scan(one_block, start, jnp.arange(blocks, dtype=jnp.int32))
    return total / features.shape[0] + 0.5 * direction

def reference(features, centers, targets):
    right_side = right_hand(features, centers, targets)
    coef = jnp.zeros_like(right_side)
    residual = right_side
    direction = right_side
    norm_now = lax.optimization_barrier(jnp.sum(residual * residual, axis=0))
    for turn in range(ITERS):
        image = apply_operator(features, centers, direction)
        curvature = lax.optimization_barrier(jnp.sum(direction * image, axis=0))
        step_size = norm_now / (curvature + 1e-06)
        coef = coef + step_size * direction
        residual = residual - step_size * image
        if turn + 1 < ITERS:
            norm_next = lax.optimization_barrier(jnp.sum(residual * residual, axis=0))
            direction = residual + norm_next / (norm_now + 1e-06) * direction
            norm_now = norm_next
    return (coef, residual)
```

```python
import functools
import math

import jax
import jax.numpy as jnp
from jax import lax
from jax.experimental import pallas as pl
from jax.experimental.pallas import tpu as pltpu
from jax.sharding import PartitionSpec as P

MESH = pl.DeviceIdType.MESH
F32, BF16 = jnp.float32, jnp.bfloat16
EPS = 1e-06


def nt(a, b):
    return lax.dot_general(a, b, (((1,), (1,)), ((), ())), preferred_element_type=F32)


def nn(a, b):
    return lax.dot_general(a, b, (((1,), (0,)), ((), ())), preferred_element_type=F32)


def total(x):
    return jnp.sum(x, axis=1, keepdims=True)


def diagonal(slot):
    lane = lax.broadcasted_iota(jnp.int32, (16, 128), 1)
    return lane == lax.broadcasted_iota(jnp.int32, (16, 128), 0) + 16 * slot


def to_row(*columns):
    held = jnp.zeros((16, 128), F32)
    for slot, column in enumerate(columns):
        held = jnp.where(diagonal(slot), column, held)
    return jnp.sum(held, axis=0, keepdims=True)


def from_row(row, slot):
    return total(jnp.where(diagonal(slot), jnp.broadcast_to(row, (16, 128)), 0.0))


def copy_to(src, dst, send, recv, where):
    return pltpu.make_async_remote_copy(
        src_ref=src, dst_ref=dst, send_sem=send, recv_sem=recv, device_id=where, device_id_type=MESH
    )


def loop(count, body):
    def step(k, carry):
        body(k)
        return carry

    lax.fori_loop(0, count, step, 0)


def kernel(
    n_total, f_ref, c_ref, t_ref, coef_ref, res_ref,
    kern, tt, part, chip, pair_in, his, hir, los, lor, bg, dg, rg,
    ps, pr, hs, hr, ph, sts, str_, wr, rems, remr, sns, snr, fins, finr, bacc, dacc, racc,
    pair_s, pair_r, hi_s, hi_r, lo_s, lo_r, ag_s, ag_r, sib_s, sib_r,
    xs_s, xs_r, cr_s, cr_r, xg_s, xg_r, st_s, st_r, w_s, w_r, rem_s, rem_r, sn_s, sn_r, fin_s, fin_r,
):
    g, j = lax.axis_index("dp"), lax.axis_index("center")
    zl, c = lax.div(g, 2), lax.rem(g, 2)
    xy, zh = lax.div(j, 2), lax.rem(j, 2)
    o = c * 8 + zl
    sibling = (zl * 2 + (1 - c), j)
    across = (g, xy * 2 + (1 - zh))

    def line(z):
        return (z * 2 + c, j)

    def any_dp(p):
        return (lax.rem(p, 8) * 2 + lax.div(p, 8), j)

    def plane(p):
        return (g, p * 2 + zh)

    def any_center(p):
        return (g, p)

    barrier = pltpu.get_barrier_semaphore()

    def greet_dp(k):
        pl.semaphore_signal(barrier, inc=1, device_id=any_dp(lax.rem(o + k + 1, 16)), device_id_type=MESH)

    def greet_center(k):
        pl.semaphore_signal(barrier, inc=1, device_id=any_center(lax.rem(j + k + 1, 32)), device_id_type=MESH)

    loop(15, greet_dp)
    loop(31, greet_center)

    scale = 0.5 / math.sqrt(f_ref.shape[1])

    def kernel_tile(k):
        rows = pl.ds(pl.multiple_of(lax.div(k, 2) * 256, 256), 256)
        cols = pl.ds(pl.multiple_of(lax.rem(k, 2) * 256, 256), 256)
        lifted = 1.0 + scale * nt(f_ref[rows, :], c_ref[cols, :])
        kern[rows, cols] = (lifted * lifted * lifted).astype(BF16)

    loop(8, kernel_tile)

    def turn_targets(k):
        at = pl.ds(pl.multiple_of(k * 256, 256), 256)
        tt[:, at] = jnp.transpose(t_ref[at, :].astype(F32)).astype(BF16)

    loop(4, turn_targets)

    def weigh(k, held):
        rows = pl.ds(pl.multiple_of(k * 64, 64), 64)
        return held + jnp.sum(kern[rows, :].astype(F32), axis=0, keepdims=True)

    wr[o] = lax.fori_loop(0, 16, weigh, jnp.zeros((1, 512), F32))

    def project(values):
        def tile(k):
            cols = pl.ds(pl.multiple_of(k * 256, 256), 256)
            part[:, :, cols] = nn(values(), kern[:, cols]).reshape(16, 16, 256)

        loop(2, tile)

    def pair_up(step):
        copy = copy_to(
            part.at[pl.ds((1 - c) * 8, 8)], pair_in.at[step], pair_s.at[step], pair_r.at[step], sibling
        )
        copy.start()
        return copy

    def pairs(copy, step):
        copy.wait()

        def add(z):
            chip[z] = part[c * 8 + z] + pair_in[step, z]

        loop(8, add)

    def along_line(src, dst, send, recv):
        def go(k):
            z = lax.rem(zl + k + 1, 8)
            copy_to(src.at[z], dst.at[zl], send.at[z], recv.at[zl], line(z)).start()

        loop(7, go)

    def line_arrived(src, dst, send, recv):
        def take(k):
            z = lax.rem(zl + k + 1, 8)
            copy_to(src.at[z], dst.at[z], send.at[z], recv.at[z], line(z)).wait()

        loop(7, take)

    def line_sum(src, dst):
        def add(k, held):
            return held + dst[lax.rem(zl + k + 1, 8)].astype(F32)

        return lax.fori_loop(0, 7, add, src[zl].astype(F32))

    def share_columns(buf, step):
        mine = buf.at[o]

        def go(k):
            z = lax.rem(zl + k + 1, 8)
            copy_to(mine, mine, ag_s.at[step, z], ag_r.at[step, zl], line(z)).start()

        loop(7, go)
        copy_to(mine, mine, sib_s.at[step, zl], sib_r.at[step, zl], sibling).start()

        def relay(k):
            z = lax.rem(zl + k + 1, 8)
            piece = buf.at[c * 8 + z]
            copy_to(piece, piece, ag_s.at[step, z], ag_r.at[step, z], line(z)).wait_recv()
            copy_to(piece, piece, sib_s.at[step, z], sib_r.at[step, z], sibling).start()

        loop(7, relay)

        def from_sibling(z):
            piece = buf.at[(1 - c) * 8 + z]
            copy_to(piece, piece, sib_s.at[step, z], sib_r.at[step, z], sibling).wait()

        loop(8, from_sibling)

        def sent(k):
            z = lax.rem(zl + k + 1, 8)
            copy_to(mine, mine, ag_s.at[step, z], ag_r.at[step, z], line(z)).wait_send()

        loop(7, sent)

    def broadcast(src, dst, me, count, send, recv, where):
        def go(k):
            p = lax.rem(me + k + 1, count)
            copy_to(src, dst.at[me], send.at[p], recv.at[me], where(p)).start()

        loop(count - 1, go)

    def scatter(src, dst, me, count, send, recv, where):
        def go(k):
            p = lax.rem(me + k + 1, count)
            copy_to(src.at[p], dst.at[me], send.at[p], recv.at[me], where(p)).start()

        loop(count - 1, go)

    def gathered(dst, me, count, send, recv, where):
        def take(k):
            p = lax.rem(me + k + 1, count)
            copy_to(dst.at[p], dst.at[p], send.at[p], recv.at[p], where(p)).wait()

        loop(count - 1, take)

    def predict(buf, step):
        def tile(k):
            cols = pl.ds(pl.multiple_of(k * 256, 256), 256)
            values = buf[...].reshape(256, 512)
            ps[step, :, :, cols] = nt(values, kern[cols, :]).astype(BF16).reshape(16, 16, 256)

        loop(4, tile)
        scatter(ps.at[step], pr.at[step], xy, 16, xs_s.at[step], xs_r.at[step], plane)
        gathered(pr.at[step], xy, 16, xs_s.at[step], xs_r.at[step], plane)

        def add(k, held):
            return held + pr[step, lax.rem(xy + k + 1, 16)].astype(F32)

        hs[step] = lax.fori_loop(0, 15, add, ps[step, xy].astype(F32)).astype(BF16)
        cross = copy_to(hs.at[step], hr.at[step], cr_s.at[step], cr_r.at[step], across)
        cross.start()
        cross.wait()
        ph[step, xy] = (hs[step].astype(F32) + hr[step].astype(F32)).astype(BF16)
        broadcast(ph.at[step, xy], ph.at[step], xy, 16, xg_s.at[step], xg_r.at[step], plane)
        gathered(ph.at[step], xy, 16, xg_s.at[step], xg_r.at[step], plane)

    def image_of(step):
        project(lambda: ph[step].reshape(256, 1024))

        def deflate(p):
            block = ph[step, p].astype(F32)
            middle = total(block) * (1.0 / block.shape[1])
            sts[step, p] = to_row(total(block * block), middle)
            part[p] = part[p] - middle * wr[o]

        loop(16, deflate)
        copy = pair_up(1 + step)
        str_[step, o] = sts[step, o]
        scatter(sts.at[step], str_.at[step], o, 16, st_s.at[step], st_r.at[step], any_dp)
        pairs(copy, 1 + step)

        def narrow(z):
            rems[step, z] = chip[z].astype(BF16)

        loop(8, narrow)
        along_line(rems.at[step], remr.at[step], rem_s.at[step], rem_r.at[step])
        gathered(str_.at[step], o, 16, st_s.at[step], st_r.at[step], any_dp)

        def add(p, held):
            return held + str_[step, p]

        squares = from_row(lax.fori_loop(0, 16, add, jnp.zeros((1, 128), F32)), 0)

        def lift(p, held):
            return held + from_row(str_[step, p], 1) * wr[p]

        lifted = lax.fori_loop(0, 16, lift, jnp.zeros((16, 512), F32))
        line_arrived(rems.at[step], remr.at[step], rem_s.at[step], rem_r.at[step])
        return line_sum(rems.at[step], remr.at[step]) + lifted, squares

    def center_start(step, *columns):
        snr[step, j] = to_row(*columns)
        broadcast(snr.at[step, j], snr.at[step], j, 32, sn_s.at[step], sn_r.at[step], any_center)

    def center_sum(step):
        gathered(snr.at[step], j, 32, sn_s.at[step], sn_r.at[step], any_center)
        return jnp.sum(snr[step].reshape(32, 128), axis=0, keepdims=True)

    project(lambda: tt[...])
    pl.semaphore_wait(barrier, 46)
    copy = pair_up(0)
    broadcast(wr.at[o], wr, o, 16, w_s, w_r, any_dp)
    pairs(copy, 0)

    def split(z):
        high = chip[z].astype(BF16)
        his[z] = high
        los[z] = (chip[z] - high.astype(F32)).astype(BF16)

    loop(8, split)
    along_line(his, hir, hi_s, hi_r)
    line_arrived(his, hir, hi_s, hi_r)
    unscale = 1.0 / math.sqrt(n_total)
    bacc[...] = line_sum(his, hir)
    bg[o] = (bacc[...] * unscale).astype(BF16)
    share_columns(bg, 0)
    along_line(los, lor, lo_s, lo_r)
    predict(bg, 0)

    line_arrived(los, lor, lo_s, lo_r)
    bacc[...] = (bacc[...] + line_sum(los, lor)) * unscale
    center_start(0, total(bacc[...] * bacc[...]))
    gathered(wr, o, 16, w_s, w_r, any_dp)
    summed, squares = image_of(0)
    norm = from_row(center_sum(0), 0)
    image = summed * (1.0 / n_total) + 0.5 * bacc[...]
    guess = norm / (squares * (1.0 / n_total) + 0.5 * norm + EPS)
    near = bacc[...] - guess * image
    center_start(1, total(bacc[...] * image), total(near * near), total(near * image), total(image * image))
    dacc[...] = image
    sums = center_sum(1)
    step_0 = norm / (from_row(sums, 0) + EPS)
    off = step_0 - guess
    norm_1 = from_row(sums, 1) - 2.0 * off * from_row(sums, 2) + off * off * from_row(sums, 3)
    racc[...] = bacc[...] - step_0 * dacc[...]
    dacc[...] = racc[...] + norm_1 / (norm + EPS) * bacc[...]
    dg[o] = dacc[...].astype(BF16)
    share_columns(dg, 1)
    center_start(2, total(dacc[...] * dacc[...]))
    predict(dg, 1)

    summed, squares = image_of(1)
    image = summed * (1.0 / n_total) + 0.5 * dacc[...]
    curvature = squares * (1.0 / n_total) + 0.5 * from_row(center_sum(2), 0)
    step_1 = norm_1 / (curvature + EPS)
    rg[o] = (racc[...] - step_1 * image).astype(BF16)
    finr[o] = to_row(step_0, step_1)
    broadcast(finr.at[o], finr, o, 16, fin_s, fin_r, any_dp)
    share_columns(rg, 2)
    gathered(finr, o, 16, fin_s, fin_r, any_dp)

    def finish(p):
        first, second = from_row(finr[p], 0), from_row(finr[p], 1)
        part[p] = first * bg[p].astype(F32) + second * dg[p].astype(F32)

    loop(16, finish)

    def turn(k):
        rows = pl.ds(pl.multiple_of(k * 128, 128), 128)
        coef_ref[rows, :] = jnp.transpose(part[:, :, rows].reshape(256, 128))
        res_ref[rows, :] = jnp.transpose(rg[:, :, rows].astype(F32).reshape(256, 128))

    loop(4, turn)


def on_device(features, centers, targets):
    n_total = features.shape[0] * lax.axis_size("dp")
    vmem, dma = pltpu.VMEM, pltpu.SemaphoreType.DMA
    whole = pl.BlockSpec(memory_space=pltpu.VMEM)
    out = jax.ShapeDtypeStruct((centers.shape[0], targets.shape[1]), F32)
    buffers = [
        vmem((1024, 512), BF16), vmem((256, 1024), BF16), vmem((16, 16, 512), F32), vmem((8, 16, 512), F32),
        vmem((3, 8, 16, 512), F32), vmem((8, 16, 512), BF16), vmem((8, 16, 512), BF16),
        vmem((8, 16, 512), BF16), vmem((8, 16, 512), BF16),
        vmem((16, 16, 512), BF16), vmem((16, 16, 512), BF16), vmem((16, 16, 512), BF16),
        vmem((2, 16, 16, 1024), BF16), vmem((2, 16, 16, 1024), BF16),
        vmem((2, 16, 1024), BF16), vmem((2, 16, 1024), BF16), vmem((2, 16, 16, 1024), BF16),
        vmem((2, 16, 1, 128), F32), vmem((2, 16, 1, 128), F32), vmem((16, 1, 512), F32),
        vmem((2, 8, 16, 512), BF16), vmem((2, 8, 16, 512), BF16),
        vmem((1, 1, 128), F32), vmem((3, 32, 1, 128), F32), vmem((1, 1, 128), F32), vmem((16, 1, 128), F32),
        vmem((16, 512), F32), vmem((16, 512), F32), vmem((16, 512), F32),
    ]
    semaphores = []
    for shape in ((3,), (8,), (8,), (3, 8), (3, 8), (2, 16), (2,), (2, 16), (2, 16), (16,), (2, 8), (3, 32), (16,)):
        semaphores += [dma(shape), dma(shape)]
    return pl.pallas_call(
        functools.partial(kernel, n_total),
        out_shape=(out, out),
        in_specs=[whole] * 3,
        out_specs=(whole, whole),
        scratch_shapes=buffers + semaphores,
        compiler_params=pltpu.CompilerParams(
            collective_id=0, has_side_effects=True, vmem_limit_bytes=40 * 1024 * 1024
        ),
    )(features, centers, targets)


def solution(mesh):
    placed = (P("dp", None), P("center", None), P("dp", None))
    return jax.shard_map(
        on_device,
        mesh=mesh,
        in_specs=placed,
        out_specs=(P("center", None), P("center", None)),
        check_vma=False,
    )
```

```python
import functools
import math

import jax
import jax.numpy as jnp
from jax import lax
from jax.experimental import pallas as pl
from jax.experimental.pallas import tpu as pltpu
from jax.sharding import PartitionSpec as P

MESH = pl.DeviceIdType.MESH
F32, BF16 = jnp.float32, jnp.bfloat16
EPS = 1e-06


def nt(a, b):
    return lax.dot_general(a, b, (((1,), (1,)), ((), ())), preferred_element_type=F32)


def nn(a, b):
    return lax.dot_general(a, b, (((1,), (0,)), ((), ())), preferred_element_type=F32)


def total(x):
    return jnp.sum(x, axis=1, keepdims=True)


def diagonal(slot):
    lane = lax.broadcasted_iota(jnp.int32, (8, 128), 1)
    return lane == lax.broadcasted_iota(jnp.int32, (8, 128), 0) + 16 * slot


def to_row(*columns):
    held = jnp.zeros((8, 128), F32)
    for slot, column in enumerate(columns):
        held = jnp.where(diagonal(slot), column, held)
    return jnp.sum(held, axis=0, keepdims=True)


def from_row(row, slot):
    return total(jnp.where(diagonal(slot), jnp.broadcast_to(row, (8, 128)), 0.0))


def copy_to(src, dst, send, recv, where):
    return pltpu.make_async_remote_copy(
        src_ref=src, dst_ref=dst, send_sem=send, recv_sem=recv, device_id=where, device_id_type=MESH
    )


def loop(count, body):
    def step(k, carry):
        body(k)
        return carry

    lax.fori_loop(0, count, step, 0)


def kernel(
    n_total, f_hbm, c_hbm, t_hbm, coef_ref, res_ref,
    f_ref, c_ref, t_ref, kern, tt, part, chip, pair_in, his, hir, los, lor, vec,
    ps, pr, hs, hr, ph, sts, str_, wr, rems, remr, snr, scn, finr, bacc, dacc, racc,
    load_f, load_c, load_t,
    pair_s, pair_r, hi_s, hi_r, lo_s, lo_r, ag_s, ag_r, sib_s, sib_r,
    xs_s, xs_r, cr_s, cr_r, xg_s, xg_r, st_s, st_r, w_s, w_r, rem_s, rem_r, sn_s, sn_r, sc_s, sc_r, fin_s, fin_r,
):
    g, j = lax.axis_index("dp"), lax.axis_index("center")
    zl, c = lax.div(g, 2), lax.rem(g, 2)
    xy, zh = lax.div(j, 2), lax.rem(j, 2)
    o = c * 8 + zl
    sibling = (zl * 2 + (1 - c), j)
    across = (g, xy * 2 + (1 - zh))

    def line(z):
        return (z * 2 + c, j)

    def any_dp(p):
        return (lax.rem(p, 8) * 2 + lax.div(p, 8), j)

    def plane(p):
        return (g, p * 2 + zh)

    barrier = pltpu.get_barrier_semaphore()

    def greet(where):
        pl.semaphore_signal(barrier, inc=1, device_id=where, device_id_type=MESH)

    greet(across)
    loop(15, lambda k: greet(any_dp(lax.rem(o + k + 1, 16))))
    loop(15, lambda k: greet(plane(lax.rem(xy + k + 1, 16))))

    scale = 0.5 / math.sqrt(f_ref.shape[1])
    unscale = 1.0 / math.sqrt(n_total)
    quarter = f_ref.shape[0] // 4

    def rows_at(k, size):
        return pl.ds(pl.multiple_of(k * size, size), size)

    def load(k):
        return pltpu.make_async_copy(f_hbm.at[rows_at(k, quarter)], f_ref.at[rows_at(k, quarter)], load_f.at[k])

    centers_in = pltpu.make_async_copy(c_hbm, c_ref, load_c)
    targets_in = pltpu.make_async_copy(t_hbm, t_ref, load_t)
    centers_in.start()
    loop(4, lambda k: load(k).start())
    targets_in.start()
    centers_in.wait()

    def kernel_rows(k):
        load(k).wait()
        rows = rows_at(k, quarter)

        def tile(i):
            cols = rows_at(i, 256)
            lifted = 1.0 + scale * nt(f_ref[rows, :], c_ref[cols, :])
            kern[rows, cols] = (lifted * lifted * lifted).astype(BF16)

        loop(2, tile)

    loop(4, kernel_rows)
    targets_in.wait()

    def turn_targets(k):
        at = rows_at(k, 256)
        turned = jnp.transpose(t_ref[at, :].astype(F32)).astype(BF16)
        tt[0, :, at] = turned[:128]
        tt[1, :, at] = turned[128:]

    loop(4, turn_targets)

    def weigh(k, held):
        return held + jnp.sum(kern[rows_at(k, 64), :].astype(F32), axis=0, keepdims=True)

    wr[o] = lax.fori_loop(0, 16, weigh, jnp.zeros((1, 512), F32))

    def project(h, values):
        def tile(k):
            cols = rows_at(k, 256)
            part[h, :, :, cols] = nn(values(), kern[:, cols]).reshape(16, 8, 256)

        loop(2, tile)

    def pair_up(h, step):
        return copy_to(
            part.at[h, pl.ds((1 - c) * 8, 8)], pair_in.at[h, step], pair_s.at[h, step], pair_r.at[h, step], sibling
        )

    def pairs(h, step):
        pair_up(h, step).wait()

        def add(z):
            chip[h, z] = part[h, c * 8 + z] + pair_in[h, step, z]

        loop(8, add)

    def along_line(src, dst, send, recv):
        def go(k):
            z = lax.rem(zl + k + 1, 8)
            copy_to(src.at[z], dst.at[zl], send.at[z], recv.at[zl], line(z)).start()

        loop(7, go)

    def line_arrived(src, dst, send, recv):
        def take(k):
            z = lax.rem(zl + k + 1, 8)
            copy_to(src.at[z], dst.at[z], send.at[z], recv.at[z], line(z)).wait()

        loop(7, take)

    def line_sum(src, dst):
        def add(k, held):
            return held + dst[lax.rem(zl + k + 1, 8)].astype(F32)

        return lax.fori_loop(0, 7, add, src[zl].astype(F32))

    def share_columns(h, step, after):
        buf, send, recv = vec.at[h, step], ag_s.at[h, step], ag_r.at[h, step]
        pair_send, pair_recv = sib_s.at[h, step], sib_r.at[h, step]
        mine = buf.at[o]

        def go(k):
            z = lax.rem(zl + k + 1, 8)
            copy_to(mine, mine, send.at[z], recv.at[zl], line(z)).start()

        loop(7, go)
        copy_to(mine, mine, pair_send.at[zl], pair_recv.at[zl], sibling).start()
        after()
        yield

        def relay(k):
            z = lax.rem(zl + k + 1, 8)
            piece = buf.at[c * 8 + z]
            copy_to(piece, piece, send.at[z], recv.at[z], line(z)).wait_recv()
            copy_to(piece, piece, pair_send.at[z], pair_recv.at[z], sibling).start()

        loop(7, relay)
        yield

        def from_sibling(z):
            piece = buf.at[(1 - c) * 8 + z]
            copy_to(piece, piece, pair_send.at[z], pair_recv.at[z], sibling).wait()

        loop(8, from_sibling)

        def sent(k):
            z = lax.rem(zl + k + 1, 8)
            copy_to(mine, mine, send.at[z], recv.at[z], line(z)).wait_send()

        loop(7, sent)

    def broadcast(src, dst, me, send, recv, where):
        def go(k):
            p = lax.rem(me + k + 1, 16)
            copy_to(src, dst.at[me], send.at[p], recv.at[me], where(p)).start()

        loop(15, go)

    def scatter(src, dst, me, send, recv, where):
        def go(k):
            p = lax.rem(me + k + 1, 16)
            copy_to(src.at[p], dst.at[me], send.at[p], recv.at[me], where(p)).start()

        loop(15, go)

    def gathered(dst, me, send, recv, where):
        def take(k):
            p = lax.rem(me + k + 1, 16)
            copy_to(dst.at[p], dst.at[p], send.at[p], recv.at[p], where(p)).wait()

        loop(15, take)

    def center_start(h, step, *columns):
        snr[h, step, xy] = to_row(*columns)
        broadcast(snr.at[h, step, xy], snr.at[h, step], xy, sn_s.at[h, step], sn_r.at[h, step], plane)

    def center_cross(h, step):
        return copy_to(scn.at[h, step, 0], scn.at[h, step, 1], sc_s.at[h, step], sc_r.at[h, step], across)

    def center_middle(h, step):
        gathered(snr.at[h, step], xy, sn_s.at[h, step], sn_r.at[h, step], plane)
        scn[h, step, 0] = jnp.sum(snr[h, step].reshape(16, 128), axis=0, keepdims=True)
        center_cross(h, step).start()

    def center_end(h, step):
        center_cross(h, step).wait()
        return scn[h, step, 0] + scn[h, step, 1]

    def predict(h, step, in_plane, in_cross):
        def tile(k):
            cols = rows_at(k, 256)
            values = vec[h, step].reshape(128, 512)
            ps[h, step, :, :, cols] = nt(values, kern[cols, :]).astype(BF16).reshape(16, 8, 256)

        loop(4, tile)
        out, back, send, recv = ps.at[h, step], pr.at[h, step], xs_s.at[h, step], xs_r.at[h, step]
        scatter(out, back, xy, send, recv, plane)
        in_plane()
        yield
        gathered(back, xy, send, recv, plane)

        def add(k, held):
            return held + pr[h, step, lax.rem(xy + k + 1, 16)].astype(F32)

        hs[h, step] = lax.fori_loop(0, 15, add, ps[h, step, xy].astype(F32)).astype(BF16)
        cross = copy_to(hs.at[h, step], hr.at[h, step], cr_s.at[h, step], cr_r.at[h, step], across)
        cross.start()
        in_cross()
        yield
        cross.wait()
        ph[h, step, xy] = (hs[h, step].astype(F32) + hr[h, step].astype(F32)).astype(BF16)
        whole, send, recv = ph.at[h, step], xg_s.at[h, step], xg_r.at[h, step]
        broadcast(whole.at[xy], whole, xy, send, recv, plane)
        yield
        gathered(whole, xy, send, recv, plane)

    waiting = [lambda: gathered(wr, o, w_s, w_r, any_dp)]

    def image_of(h, step):
        project(h, lambda: ph[h, step].reshape(128, 1024))

        def deflate(p):
            block = ph[h, step, p].astype(F32)
            middle = total(block) * (1.0 / block.shape[1])
            sts[h, step, p] = to_row(total(block * block), middle)
            part[h, p] = part[h, p] - middle * wr[o]

        loop(16, deflate)
        pair_up(h, 1 + step).start()
        str_[h, step, o] = sts[h, step, o]
        stats = str_.at[h, step], o, st_s.at[h, step], st_r.at[h, step], any_dp
        scatter(sts.at[h, step], *stats)
        yield
        pairs(h, 1 + step)

        def narrow(z):
            rems[h, step, z] = chip[h, z].astype(BF16)

        loop(8, narrow)
        moved = rems.at[h, step], remr.at[h, step], rem_s.at[h, step], rem_r.at[h, step]
        along_line(*moved)
        yield
        while waiting:
            waiting.pop()()
        gathered(*stats)

        def add(p, held):
            return held + str_[h, step, p]

        squares = from_row(lax.fori_loop(0, 16, add, jnp.zeros((1, 128), F32)), 0)

        def lift(p, held):
            return held + from_row(str_[h, step, p], 1) * wr[p]

        lifted = lax.fori_loop(0, 16, lift, jnp.zeros((8, 512), F32))
        line_arrived(*moved)
        summed = line_sum(moved[0], moved[1]) + lifted
        return summed * (1.0 / n_total), squares * (1.0 / n_total)

    def chain(h):
        project(h, lambda: tt[h])
        yield
        pair_up(h, 0).start()
        yield
        pairs(h, 0)

        def split(z):
            high = chip[h, z].astype(BF16)
            his[h, z] = high
            los[h, z] = (chip[h, z] - high.astype(F32)).astype(BF16)

        loop(8, split)
        highs = his.at[h], hir.at[h], hi_s.at[h], hi_r.at[h]
        lows = los.at[h], lor.at[h], lo_s.at[h], lo_r.at[h]
        along_line(*highs)
        yield
        line_arrived(*highs)
        bacc[h] = line_sum(highs[0], highs[1])
        vec[h, 0, o] = (bacc[h] * unscale).astype(BF16)
        yield from share_columns(h, 0, lambda: along_line(*lows))

        def finish_right_side():
            line_arrived(*lows)
            bacc[h] = (bacc[h] + line_sum(lows[0], lows[1])) * unscale
            center_start(h, 0, total(bacc[h] * bacc[h]))

        yield from predict(h, 0, finish_right_side, lambda: center_middle(h, 0))
        summed, squares = yield from image_of(h, 0)
        norm = from_row(center_end(h, 0), 0)
        image = summed + 0.5 * bacc[h]
        guess = norm / (squares + 0.5 * norm + EPS)
        near = bacc[h] - guess * image
        dacc[h] = image
        center_start(h, 1, total(bacc[h] * image), total(near * near), total(near * image), total(image * image))
        yield
        center_middle(h, 1)
        yield
        sums = center_end(h, 1)
        step_0 = norm / (from_row(sums, 0) + EPS)
        off = step_0 - guess
        norm_1 = from_row(sums, 1) - 2.0 * off * from_row(sums, 2) + off * off * from_row(sums, 3)
        racc[h] = bacc[h] - step_0 * dacc[h]
        dacc[h] = racc[h] + norm_1 / (norm + EPS) * bacc[h]
        vec[h, 1, o] = dacc[h].astype(BF16)
        yield from share_columns(h, 1, lambda: center_start(h, 2, total(dacc[h] * dacc[h])))
        yield from predict(h, 1, lambda: center_middle(h, 2), lambda: None)
        summed, squares = yield from image_of(h, 1)
        image = summed + 0.5 * dacc[h]
        step_1 = norm_1 / (squares + 0.5 * from_row(center_end(h, 2), 0) + EPS)
        vec[h, 2, o] = (racc[h] - step_1 * image).astype(BF16)
        finr[h, o] = to_row(step_0, step_1)
        final = finr.at[h], o, fin_s.at[h], fin_r.at[h], any_dp
        yield from share_columns(h, 2, lambda: broadcast(finr.at[h, o], *final))
        gathered(*final)

        def finish(p):
            first, second = from_row(finr[h, p], 0), from_row(finr[h, p], 1)
            part[h, p] = first * vec[h, 0, p].astype(F32) + second * vec[h, 1, p].astype(F32)

        loop(16, finish)

        def turn(k):
            rows = rows_at(k, 128)
            cols = pl.ds(h * 128, 128)
            coef_ref[rows, cols] = jnp.transpose(part[h, :, :, rows].reshape(128, 128))
            res_ref[rows, cols] = jnp.transpose(vec[h, 2, :, :, rows].astype(F32).reshape(128, 128))

        loop(4, turn)

    chains = [chain(0), chain(1)]
    for half in chains:
        next(half)
    pl.semaphore_wait(barrier, 31)
    started = False
    while chains:
        for half in list(chains):
            if next(half, "done") == "done":
                chains.remove(half)
        if not started:
            broadcast(wr.at[o], wr, o, w_s, w_r, any_dp)
            started = True


def on_device(features, centers, targets):
    n_total = features.shape[0] * lax.axis_size("dp")
    vmem, dma = pltpu.VMEM, pltpu.SemaphoreType.DMA
    whole = pl.BlockSpec(memory_space=pltpu.VMEM)
    out = jax.ShapeDtypeStruct((centers.shape[0], targets.shape[1]), F32)
    buffers = [
        vmem((1024, 1024), BF16), vmem((512, 1024), BF16), vmem((1024, 256), BF16),
        vmem((1024, 512), BF16), vmem((2, 128, 1024), BF16), vmem((2, 16, 8, 512), F32), vmem((2, 8, 8, 512), F32),
        vmem((2, 3, 8, 8, 512), F32), vmem((2, 8, 8, 512), BF16), vmem((2, 8, 8, 512), BF16),
        vmem((2, 8, 8, 512), BF16), vmem((2, 8, 8, 512), BF16), vmem((2, 3, 16, 8, 512), BF16),
        vmem((2, 2, 16, 8, 1024), BF16), vmem((2, 2, 16, 8, 1024), BF16),
        vmem((2, 2, 8, 1024), BF16), vmem((2, 2, 8, 1024), BF16), vmem((2, 2, 16, 8, 1024), BF16),
        vmem((2, 2, 16, 1, 128), F32), vmem((2, 2, 16, 1, 128), F32), vmem((16, 1, 512), F32),
        vmem((2, 2, 8, 8, 512), BF16), vmem((2, 2, 8, 8, 512), BF16),
        vmem((2, 3, 16, 1, 128), F32), vmem((2, 3, 2, 1, 128), F32), vmem((2, 16, 1, 128), F32),
        vmem((2, 8, 512), F32), vmem((2, 8, 512), F32), vmem((2, 8, 512), F32),
        dma((4,)), dma, dma,
    ]
    semaphores = []
    for shape in (
        (2, 3), (2, 8), (2, 8), (2, 3, 8), (2, 3, 8), (2, 2, 16), (2, 2), (2, 2, 16), (2, 2, 16), (16,),
        (2, 2, 8), (2, 3, 16), (2, 3), (2, 16),
    ):
        semaphores += [dma(shape), dma(shape)]
    return pl.pallas_call(
        functools.partial(kernel, n_total),
        out_shape=(out, out),
        in_specs=[pl.BlockSpec(memory_space=pl.ANY)] * 3,
        out_specs=(whole, whole),
        scratch_shapes=buffers + semaphores,
        compiler_params=pltpu.CompilerParams(
            collective_id=0, has_side_effects=True, vmem_limit_bytes=60 * 1024 * 1024
        ),
    )(features, centers, targets)


def solution(mesh):
    placed = (P("dp", None), P("center", None), P("dp", None))
    return jax.shard_map(
        on_device,
        mesh=mesh,
        in_specs=placed,
        out_specs=(P("center", None), P("center", None)),
        check_vma=False,
    )
```

```python
import functools
import math

import jax
import jax.numpy as jnp
from jax import lax
from jax.experimental import pallas as pl
from jax.experimental.pallas import tpu as pltpu
from jax.sharding import PartitionSpec as P

MESH = pl.DeviceIdType.MESH
F32, BF16 = jnp.float32, jnp.bfloat16
EPS = 1e-06
FIRST = 2


def nt(a, b):
    return lax.dot_general(a, b, (((1,), (1,)), ((), ())), preferred_element_type=F32)


def nn(a, b):
    return lax.dot_general(a, b, (((1,), (0,)), ((), ())), preferred_element_type=F32)


def total(x):
    return jnp.sum(x, axis=1, keepdims=True)


def diagonal(slot):
    lane = lax.broadcasted_iota(jnp.int32, (16, 128), 1)
    return lane == lax.broadcasted_iota(jnp.int32, (16, 128), 0) + 16 * slot


def to_row(*columns):
    held = jnp.zeros((16, 128), F32)
    for slot, column in enumerate(columns):
        held = jnp.where(diagonal(slot), column, held)
    return jnp.sum(held, axis=0, keepdims=True)


def from_row(row, slot):
    return total(jnp.where(diagonal(slot), jnp.broadcast_to(row, (16, 128)), 0.0))


def to_rows(*columns):
    held = jnp.zeros((8, 16, 128), F32)
    for slot, column in enumerate(columns):
        held = jnp.where(diagonal(slot)[None], column, held)
    return jnp.sum(held, axis=1, keepdims=True)


def from_rows(rows, slot):
    spread = jnp.where(diagonal(slot)[None], jnp.broadcast_to(rows, (rows.shape[0], 16, 128)), 0.0)
    return jnp.sum(spread, axis=2, keepdims=True)


def copy_to(src, dst, send, recv, where):
    return pltpu.make_async_remote_copy(
        src_ref=src, dst_ref=dst, send_sem=send, recv_sem=recv, device_id=where, device_id_type=MESH
    )


def loop(count, body):
    def step(k, carry):
        body(k)
        return carry

    lax.fori_loop(0, count, step, 0)


def kernel(
    n_total, f_hbm, c_hbm, t_hbm, coef_ref, res_ref,
    f_ref, c_ref, t_ref, kern, flip, tt, part, pair_in, his, hir, los, lor, vec,
    ps, pr, hs, hr, ph, sts, str_, wr, rems, remr, snr, scn, finr, bacc, dacc, racc, held,
    load_f, load_c, load_t,
    pair_s, pair_r, hi_s, hi_r, lo_s, lo_r, ag_s, ag_r, sib_s, sib_r,
    xs_s, xs_r, cr_s, cr_r, xg_s, xg_r, st_s, st_r, w_s, w_r, rem_s, rem_r, sn_s, sn_r, sc_s, sc_r, fin_s, fin_r,
):
    g, j = lax.axis_index("dp"), lax.axis_index("center")
    zl, c = lax.div(g, 2), lax.rem(g, 2)
    xy, zh = lax.div(j, 2), lax.rem(j, 2)
    me = c * 8 + zl
    owning = jnp.logical_and(zl >= FIRST, zl < FIRST + 4)
    seat = lax.clamp(0, zl - FIRST, 3)
    o = c * 4 + seat
    sibling = (zl * 2 + (1 - c), j)
    across = (g, xy * 2 + (1 - zh))

    def line(z):
        return (z * 2 + c, j)

    def any_dp(p):
        return (lax.rem(p, 8) * 2 + lax.div(p, 8), j)

    def owner_at(q):
        return lax.div(q, 4) * 8 + FIRST + lax.rem(q, 4)

    def plane(p):
        return (g, p * 2 + zh)

    barrier = pltpu.get_barrier_semaphore()

    def greet(where):
        pl.semaphore_signal(barrier, inc=1, device_id=where, device_id_type=MESH)

    greet(across)
    loop(15, lambda k: greet(any_dp(lax.rem(me + k + 1, 16))))
    loop(15, lambda k: greet(plane(lax.rem(xy + k + 1, 16))))

    scale = 0.5 / math.sqrt(f_ref.shape[1])
    unscale = 1.0 / math.sqrt(n_total)
    quarter = f_ref.shape[0] // 4

    def rows_at(k, size):
        return pl.ds(pl.multiple_of(k * size, size), size)

    def load(k):
        return pltpu.make_async_copy(f_hbm.at[rows_at(k, quarter)], f_ref.at[rows_at(k, quarter)], load_f.at[k])

    centers_in = pltpu.make_async_copy(c_hbm, c_ref, load_c)
    targets_in = pltpu.make_async_copy(t_hbm, t_ref, load_t)
    centers_in.start()
    loop(4, lambda k: load(k).start())
    targets_in.start()
    centers_in.wait()

    def kernel_rows(k):
        load(k).wait()
        rows = rows_at(k, quarter)

        def tile(i):
            cols = rows_at(i, 256)
            lifted = 1.0 + scale * nt(f_ref[rows, :], c_ref[cols, :])
            cubed = lifted * lifted * lifted
            kern[rows, cols] = cubed.astype(BF16)
            flip[cols, rows] = jnp.transpose(cubed).astype(BF16)

        loop(2, tile)

    loop(4, kernel_rows)
    targets_in.wait()

    def turn_targets(k):
        at = rows_at(k, 256)
        turned = jnp.transpose(t_ref[at, :].astype(F32)).astype(BF16)
        tt[0, :, at] = turned[:128]
        tt[1, :, at] = turned[128:]

    loop(4, turn_targets)

    def weigh(k, held):
        return held + jnp.sum(kern[rows_at(k, 64), :].astype(F32), axis=0, keepdims=True)

    wr[me] = lax.fori_loop(0, 16, weigh, jnp.zeros((1, 512), F32))

    def project(h, values):
        def tile(k):
            cols = rows_at(k, 256)
            part[h, :, :, cols] = nn(values(), kern[:, cols]).reshape(8, 16, 256)

        loop(2, tile)

    def pair_up(h, step):
        return copy_to(
            part.at[h, pl.ds((1 - c) * 4, 4)], pair_in.at[h, step], pair_s.at[h, step], pair_r.at[h, step], sibling
        )

    def pairs(h, step):
        pair_up(h, step).wait()
        return part[h, pl.ds(c * 4, 4)] + pair_in[h, step]

    def others(count, first, body):
        def visit(k):
            z = first + k

            @pl.when(z != zl)
            def _():
                body(k, z)

        loop(count, visit)

    def to_owners(src, dst, send, recv):
        def go(k, z):
            copy_to(src.at[k], dst.at[zl], send.at[k], recv.at[zl], line(z)).start()

        others(4, FIRST, go)

    def owners_took(src, dst, send, recv):
        def gone(k, z):
            copy_to(src.at[k], dst.at[zl], send.at[k], recv.at[zl], line(z)).wait_send()

        others(4, FIRST, gone)

    def line_sum(src, dst, send, recv):
        def take(k, z):
            copy_to(dst.at[z], dst.at[z], send.at[0], recv.at[z], line(z)).wait_recv()

        others(8, 0, take)
        dst[zl] = src[seat]
        return jnp.sum(dst[...].astype(F32), axis=0)

    def share_columns(h, step, after):
        buf, send, recv = vec.at[h, step], ag_s.at[h, step], ag_r.at[h, step]
        pair_send, pair_recv = sib_s.at[h, step], sib_r.at[h, step]
        mine = buf.at[o]

        @pl.when(owning)
        def _():
            def go(k, z):
                copy_to(mine, mine, send.at[z], recv.at[seat], line(z)).start()

            others(8, 0, go)
            copy_to(mine, mine, pair_send.at[seat], pair_recv.at[seat], sibling).start()
            after()

        yield

        def relay(k, z):
            piece = buf.at[c * 4 + k]
            copy_to(piece, piece, send.at[z], recv.at[k], line(z)).wait_recv()
            copy_to(piece, piece, pair_send.at[k], pair_recv.at[k], sibling).start()

        others(4, FIRST, relay)
        yield

        def from_sibling(k):
            piece = buf.at[(1 - c) * 4 + k]
            copy_to(piece, piece, pair_send.at[k], pair_recv.at[k], sibling).wait()

        loop(4, from_sibling)

        @pl.when(owning)
        def _():
            def sent(k, z):
                copy_to(mine, mine, send.at[z], recv.at[seat], line(z)).wait_send()

            others(8, 0, sent)

    def tell_owners(src, dst, send, recv):
        def go(q):
            p = owner_at(q)

            @pl.when(p != me)
            def _():
                copy_to(src(q), dst.at[me], send.at[q], recv.at[me], any_dp(p)).start()

        loop(8, go)

    def owners_told(src, dst, send, recv):
        def gone(q):
            p = owner_at(q)

            @pl.when(p != me)
            def _():
                copy_to(src(q), dst.at[me], send.at[q], recv.at[me], any_dp(p)).wait_send()

        loop(8, gone)

        @pl.when(owning)
        def _():
            def take(k):
                p = lax.rem(me + k + 1, 16)
                copy_to(dst.at[p], dst.at[p], send.at[0], recv.at[p], any_dp(p)).wait_recv()

            loop(15, take)

    def broadcast(src, dst, own, send, recv, where):
        def go(k):
            p = lax.rem(own + k + 1, 16)
            copy_to(src, dst.at[own], send.at[p], recv.at[own], where(p)).start()

        loop(15, go)

    def scatter(src, dst, own, send, recv, where):
        def go(k):
            p = lax.rem(own + k + 1, 16)
            copy_to(src.at[p], dst.at[own], send.at[p], recv.at[own], where(p)).start()

        loop(15, go)

    def gathered(dst, own, send, recv, where):
        def take(k):
            p = lax.rem(own + k + 1, 16)
            copy_to(dst.at[p], dst.at[p], send.at[p], recv.at[p], where(p)).wait()

        loop(15, take)

    def center_start(h, step, *columns):
        snr[h, step, xy] = to_row(*columns)
        broadcast(snr.at[h, step, xy], snr.at[h, step], xy, sn_s.at[h, step], sn_r.at[h, step], plane)

    def center_cross(h, step):
        return copy_to(scn.at[h, step, 0], scn.at[h, step, 1], sc_s.at[h, step], sc_r.at[h, step], across)

    def center_middle(h, step):
        gathered(snr.at[h, step], xy, sn_s.at[h, step], sn_r.at[h, step], plane)
        scn[h, step, 0] = jnp.sum(snr[h, step].reshape(16, 128), axis=0, keepdims=True)
        center_cross(h, step).start()

    def center_end(h, step):
        center_cross(h, step).wait()
        return scn[h, step, 0] + scn[h, step, 1]

    def predict(h, step, in_plane, in_cross):
        def tile(k):
            cols = rows_at(k, 256)
            values = vec[h, step].reshape(128, 512)
            ps[h, step, :, :, cols] = nn(values, flip[:, cols]).astype(BF16).reshape(16, 8, 256)

        loop(4, tile)
        out, back, send, recv = ps.at[h, step], pr.at[h, step], xs_s.at[h, step], xs_r.at[h, step]
        scatter(out, back, xy, send, recv, plane)
        in_plane()
        yield
        gathered(back, xy, send, recv, plane)

        pr[h, step, xy] = ps[h, step, xy]
        hs[h, step] = jnp.sum(pr[h, step].astype(F32), axis=0).astype(BF16)
        cross = copy_to(hs.at[h, step], hr.at[h, step], cr_s.at[h, step], cr_r.at[h, step], across)
        cross.start()
        in_cross()
        yield
        cross.wait()
        ph[h, step, xy] = (hs[h, step].astype(F32) + hr[h, step].astype(F32)).astype(BF16)
        whole, send, recv = ph.at[h, step], xg_s.at[h, step], xg_r.at[h, step]
        broadcast(whole.at[xy], whole, xy, send, recv, plane)
        yield
        gathered(whole, xy, send, recv, plane)

    weights = lambda q: wr.at[me], wr, w_s, w_r
    waiting = [lambda: owners_told(*weights)]

    def keep(h, slot, value):
        held[h, slot] = jnp.broadcast_to(value, (16, 128))

    def kept(h, slot):
        return held[h, slot][:, :1]

    def image_of(h, step, use):
        project(h, lambda: ph[h, step].reshape(128, 1024))
        block = ph[h, step].astype(F32).reshape(8, 16, 1024)
        middle = jnp.sum(block, axis=2, keepdims=True) * (1.0 / block.shape[2])
        sts[h, step] = to_rows(jnp.sum(block * block, axis=2, keepdims=True), middle)
        part[h] = part[h] - middle * wr[me][None]
        pair_up(h, 1 + step).start()
        told = str_.at[h, step]
        stats = lambda q: sts.at[h, step, q], told, st_s.at[h, step], st_r.at[h, step]
        tell_owners(*stats)
        yield
        rems[h, step] = pairs(h, 1 + step).astype(BF16)
        moved = rems.at[h, step], remr.at[h, step], rem_s.at[h, step], rem_r.at[h, step]
        to_owners(*moved)
        yield
        while waiting:
            waiting.pop()()
        owners_told(*stats)

        @pl.when(owning)
        def _():
            told[me] = sts[h, step, o]
            rows = told[...]
            squares = from_row(jnp.sum(rows, axis=0), 0)
            lifted = jnp.sum(from_rows(rows, 1) * wr[...], axis=0)
            use((line_sum(*moved) + lifted) * (1.0 / n_total), squares * (1.0 / n_total))

        owners_took(*moved)

    def chain(h):
        project(h, lambda: tt[h])
        yield
        pair_up(h, 0).start()
        yield
        both = pairs(h, 0)
        high = both.astype(BF16)
        his[h] = high
        los[h] = (both - high.astype(F32)).astype(BF16)
        highs = his.at[h], hir.at[h], hi_s.at[h], hi_r.at[h]
        lows = los.at[h], lor.at[h], lo_s.at[h], lo_r.at[h]
        to_owners(*highs)
        yield

        @pl.when(owning)
        def _():
            bacc[h] = line_sum(*highs)
            vec[h, 0, o] = (bacc[h] * unscale).astype(BF16)

        yield from share_columns(h, 0, lambda: None)
        owners_took(*highs)

        def finish_right_side():
            @pl.when(owning)
            def _():
                bacc[h] = (bacc[h] + line_sum(*lows)) * unscale
                center_start(h, 0, total(bacc[h] * bacc[h]))

            owners_took(*lows)

        yield from predict(h, 0, lambda: to_owners(*lows), finish_right_side)

        def open_first(summed, squares):
            norm = from_row(center_end(h, 0), 0)
            image = summed + 0.5 * bacc[h]
            guess = norm / (squares + 0.5 * norm + EPS)
            near = bacc[h] - guess * image
            dacc[h] = image
            keep(h, 0, norm)
            keep(h, 1, guess)
            center_start(h, 1, total(bacc[h] * image), total(near * near), total(near * image), total(image * image))

        pl.when(owning)(lambda: center_middle(h, 0))
        yield from image_of(h, 0, open_first)
        yield
        pl.when(owning)(lambda: center_middle(h, 1))
        yield

        @pl.when(owning)
        def _():
            sums = center_end(h, 1)
            norm, guess = kept(h, 0), kept(h, 1)
            step_0 = norm / (from_row(sums, 0) + EPS)
            off = step_0 - guess
            norm_1 = from_row(sums, 1) - 2.0 * off * from_row(sums, 2) + off * off * from_row(sums, 3)
            racc[h] = bacc[h] - step_0 * dacc[h]
            dacc[h] = racc[h] + norm_1 / (norm + EPS) * bacc[h]
            vec[h, 1, o] = dacc[h].astype(BF16)
            keep(h, 2, step_0)
            keep(h, 3, norm_1)

        yield from share_columns(h, 1, lambda: center_start(h, 2, total(dacc[h] * dacc[h])))
        yield from predict(h, 1, lambda: pl.when(owning)(lambda: center_middle(h, 2)), lambda: None)
        send_all, recv_all = fin_s.at[h], fin_r.at[h]

        def close(summed, squares):
            image = summed + 0.5 * dacc[h]
            step_1 = kept(h, 3) / (squares + 0.5 * from_row(center_end(h, 2), 0) + EPS)
            vec[h, 2, o] = (racc[h] - step_1 * image).astype(BF16)
            finr[h, o] = to_row(kept(h, 2), step_1)

        def announce():
            def go(k):
                p = lax.rem(me + k + 1, 16)
                copy_to(finr.at[h, o], finr.at[h, o], send_all.at[p], recv_all.at[o], any_dp(p)).start()

            loop(15, go)

        yield from image_of(h, 1, close)
        yield from share_columns(h, 2, announce)

        def hear(q):
            p = owner_at(q)

            @pl.when(p != me)
            def _():
                copy_to(finr.at[h, q], finr.at[h, q], send_all.at[p], recv_all.at[q], any_dp(p)).wait_recv()

        loop(8, hear)

        @pl.when(owning)
        def _():
            def sent(k):
                p = lax.rem(me + k + 1, 16)
                copy_to(finr.at[h, o], finr.at[h, o], send_all.at[p], recv_all.at[o], any_dp(p)).wait_send()

            loop(15, sent)

        first, second = from_rows(finr[h], 0), from_rows(finr[h], 1)
        part[h] = first * vec[h, 0].astype(F32) + second * vec[h, 1].astype(F32)

        def turn(k):
            rows = rows_at(k, 128)
            cols = pl.ds(h * 128, 128)
            coef_ref[rows, cols] = jnp.transpose(part[h, :, :, rows].reshape(128, 128))
            res_ref[rows, cols] = jnp.transpose(vec[h, 2, :, :, rows].astype(F32).reshape(128, 128))

        loop(4, turn)

    chains = [chain(0), chain(1)]
    for half in chains:
        next(half)
    pl.semaphore_wait(barrier, 31)
    started = False
    while chains:
        for half in list(chains):
            if next(half, "done") == "done":
                chains.remove(half)
        if not started:
            tell_owners(*weights)
            started = True


def on_device(features, centers, targets):
    n_total = features.shape[0] * lax.axis_size("dp")
    vmem, dma = pltpu.VMEM, pltpu.SemaphoreType.DMA
    whole = pl.BlockSpec(memory_space=pltpu.VMEM)
    out = jax.ShapeDtypeStruct((centers.shape[0], targets.shape[1]), F32)
    buffers = [
        vmem((1024, 1024), BF16), vmem((512, 1024), BF16), vmem((1024, 256), BF16),
        vmem((1024, 512), BF16), vmem((512, 1024), BF16), vmem((2, 128, 1024), BF16), vmem((2, 8, 16, 512), F32),
        vmem((2, 3, 4, 16, 512), F32), vmem((2, 4, 16, 512), BF16), vmem((2, 8, 16, 512), BF16),
        vmem((2, 4, 16, 512), BF16), vmem((2, 8, 16, 512), BF16), vmem((2, 3, 8, 16, 512), BF16),
        vmem((2, 2, 16, 8, 1024), BF16), vmem((2, 2, 16, 8, 1024), BF16),
        vmem((2, 2, 8, 1024), BF16), vmem((2, 2, 8, 1024), BF16), vmem((2, 2, 16, 8, 1024), BF16),
        vmem((2, 2, 8, 1, 128), F32), vmem((2, 2, 16, 1, 128), F32), vmem((16, 1, 512), F32),
        vmem((2, 2, 4, 16, 512), BF16), vmem((2, 2, 8, 16, 512), BF16),
        vmem((2, 3, 16, 1, 128), F32), vmem((2, 3, 2, 1, 128), F32), vmem((2, 8, 1, 128), F32),
        vmem((2, 16, 512), F32), vmem((2, 16, 512), F32), vmem((2, 16, 512), F32), vmem((2, 4, 16, 128), F32),
        dma((4,)), dma, dma,
    ]
    semaphores = []
    for send, recv in (
        ((2, 3), (2, 3)), ((2, 4), (2, 8)), ((2, 4), (2, 8)), ((2, 3, 8), (2, 3, 4)), ((2, 3, 4), (2, 3, 4)),
        ((2, 2, 16), (2, 2, 16)), ((2, 2), (2, 2)), ((2, 2, 16), (2, 2, 16)), ((2, 2, 8), (2, 2, 16)), ((8,), (16,)),
        ((2, 2, 4), (2, 2, 8)), ((2, 3, 16), (2, 3, 16)), ((2, 3), (2, 3)), ((2, 16), (2, 8)),
    ):
        semaphores += [dma(send), dma(recv)]
    return pl.pallas_call(
        functools.partial(kernel, n_total),
        out_shape=(out, out),
        in_specs=[pl.BlockSpec(memory_space=pl.ANY)] * 3,
        out_specs=(whole, whole),
        scratch_shapes=buffers + semaphores,
        compiler_params=pltpu.CompilerParams(
            collective_id=0, has_side_effects=True, vmem_limit_bytes=60 * 1024 * 1024
        ),
    )(features, centers, targets)


def solution(mesh):
    placed = (P("dp", None), P("center", None), P("dp", None))
    return jax.shard_map(
        on_device,
        mesh=mesh,
        in_specs=placed,
        out_specs=(P("center", None), P("center", None)),
        check_vma=False,
    )
```

```python
import functools
import math

import jax
import jax.numpy as jnp
from jax import lax
from jax.experimental import pallas as pl
from jax.experimental.pallas import tpu as pltpu
from jax.sharding import PartitionSpec as P

MESH = pl.DeviceIdType.MESH
F32, BF16 = jnp.float32, jnp.bfloat16
EPS = 1e-06
FAR_FIRST = sorted(
    ((a, b) for a in range(4) for b in range(4) if a + b), key=lambda t: -min(t[0], 4 - t[0]) - min(t[1], 4 - t[1])
)
FIRST = 2


def nt(a, b):
    return lax.dot_general(a, b, (((1,), (1,)), ((), ())), preferred_element_type=F32)


def nn(a, b):
    return lax.dot_general(a, b, (((1,), (0,)), ((), ())), preferred_element_type=F32)


def total(x):
    return jnp.sum(x, axis=1, keepdims=True)


def diagonal(slot):
    lane = lax.broadcasted_iota(jnp.int32, (16, 128), 1)
    return lane == lax.broadcasted_iota(jnp.int32, (16, 128), 0) + 16 * slot


def to_row(*columns):
    held = jnp.zeros((16, 128), F32)
    for slot, column in enumerate(columns):
        held = jnp.where(diagonal(slot), column, held)
    return jnp.sum(held, axis=0, keepdims=True)


def from_row(row, slot):
    return total(jnp.where(diagonal(slot), jnp.broadcast_to(row, (16, 128)), 0.0))


def to_rows(*columns):
    held = jnp.zeros((8, 16, 128), F32)
    for slot, column in enumerate(columns):
        held = jnp.where(diagonal(slot)[None], column, held)
    return jnp.sum(held, axis=1, keepdims=True)


def from_rows(rows, slot):
    spread = jnp.where(diagonal(slot)[None], jnp.broadcast_to(rows, (rows.shape[0], 16, 128)), 0.0)
    return jnp.sum(spread, axis=2, keepdims=True)


def copy_to(src, dst, send, recv, where):
    return pltpu.make_async_remote_copy(
        src_ref=src, dst_ref=dst, send_sem=send, recv_sem=recv, device_id=where, device_id_type=MESH
    )


def loop(count, body):
    def step(k, carry):
        body(k)
        return carry

    lax.fori_loop(0, count, step, 0)


def kernel(
    n_total, f_hbm, c_hbm, t_hbm, coef_ref, res_ref,
    f_ref, c_ref, t_ref, kern, flip, tt, part, pair_in, his, hir, los, lor, vec,
    ps, pr, hs, hr, ph, sts, str_, wr, rems, remr, snr, scn, finr, bacc, dacc, racc, held,
    load_f, load_c, load_t,
    pair_s, pair_r, hi_s, hi_r, lo_s, lo_r, ag_s, ag_r, sib_s, sib_r,
    xs_s, xs_r, cr_s, cr_r, xg_s, xg_r, st_s, st_r, w_s, w_r, rem_s, rem_r, sn_s, sn_r, sc_s, sc_r, fin_s, fin_r,
):
    g, j = lax.axis_index("dp"), lax.axis_index("center")
    zl, c = lax.div(g, 2), lax.rem(g, 2)
    xy, zh = lax.div(j, 2), lax.rem(j, 2)
    me = c * 8 + zl
    owning = jnp.logical_and(zl >= FIRST, zl < FIRST + 4)
    seat = lax.clamp(0, zl - FIRST, 3)
    o = c * 4 + seat
    sibling = (zl * 2 + (1 - c), j)
    across = (g, xy * 2 + (1 - zh))

    def line(z):
        return (z * 2 + c, j)

    def any_dp(p):
        return (lax.rem(p, 8) * 2 + lax.div(p, 8), j)

    def owner_at(q):
        return lax.div(q, 4) * 8 + FIRST + lax.rem(q, 4)

    def plane(p):
        return (g, p * 2 + zh)

    barrier = pltpu.get_barrier_semaphore()

    def greet(where):
        pl.semaphore_signal(barrier, inc=1, device_id=where, device_id_type=MESH)

    greet(across)
    loop(15, lambda k: greet(any_dp(lax.rem(me + k + 1, 16))))
    loop(15, lambda k: greet(plane(lax.rem(xy + k + 1, 16))))

    scale = 0.5 / math.sqrt(f_ref.shape[1])
    unscale = 1.0 / math.sqrt(n_total)
    quarter = f_ref.shape[0] // 4

    def rows_at(k, size):
        return pl.ds(pl.multiple_of(k * size, size), size)

    def load(k):
        return pltpu.make_async_copy(f_hbm.at[rows_at(k, quarter)], f_ref.at[rows_at(k, quarter)], load_f.at[k])

    centers_in = pltpu.make_async_copy(c_hbm, c_ref, load_c)
    targets_in = pltpu.make_async_copy(t_hbm, t_ref, load_t)
    centers_in.start()
    loop(4, lambda k: load(k).start())
    targets_in.start()
    centers_in.wait()

    def kernel_rows(k):
        load(k).wait()
        rows = rows_at(k, quarter)

        def tile(i):
            cols = rows_at(i, 256)
            lifted = 1.0 + scale * nt(f_ref[rows, :], c_ref[cols, :])
            kern[rows, cols] = (lifted * lifted * lifted).astype(BF16)

        loop(2, tile)

    loop(4, kernel_rows)
    targets_in.wait()

    def turn_targets(k):
        at = rows_at(k, 256)
        turned = jnp.transpose(t_ref[at, :].astype(F32)).astype(BF16)
        tt[0, :, at] = turned[:128]
        tt[1, :, at] = turned[128:]

    loop(4, turn_targets)

    def weigh(k, held):
        return held + jnp.sum(kern[rows_at(k, 64), :].astype(F32), axis=0, keepdims=True)

    def prepare():
        def turn_kernel(k):
            rows = rows_at(k, 128)
            flip[:, rows] = jnp.transpose(kern[rows, :].astype(F32)).astype(BF16)

        loop(8, turn_kernel)
        wr[me] = lax.fori_loop(0, 16, weigh, jnp.zeros((1, 512), F32))
        tell_owners(*weights)

    def project(h, values):
        def tile(k):
            cols = rows_at(k, 256)
            part[h, :, :, cols] = nn(values(), kern[:, cols]).reshape(8, 16, 256)

        loop(2, tile)

    def pair_up(h, step):
        return copy_to(
            part.at[h, pl.ds((1 - c) * 4, 4)], pair_in.at[h, step], pair_s.at[h, step], pair_r.at[h, step], sibling
        )

    def pairs(h, step):
        pair_up(h, step).wait()
        return part[h, pl.ds(c * 4, 4)] + pair_in[h, step]

    def others(count, first, body):
        def visit(k):
            z = first + k

            @pl.when(z != zl)
            def _():
                body(k, z)

        loop(count, visit)

    def farthest_first(reach, low, high, body):
        def visit(k):
            for z in (zl + reach - k, zl - reach + k):

                @pl.when(jnp.logical_and(z >= low, z < high))
                def _():
                    body(z)

        loop(reach, visit)

    def to_owners(src, dst, send, recv):
        def go(z):
            k = z - FIRST
            copy_to(src.at[k], dst.at[zl], send, recv, line(z)).start()

        farthest_first(5, FIRST, FIRST + 4, go)

    def sent_or_told(count, wait):
        pl.when(owning)(lambda: wait(count - 1))
        pl.when(jnp.logical_not(owning))(lambda: wait(count))

    def many(ref, count, send, recv):
        rows = ref.at[pl.ds(0, count)]
        return copy_to(rows, rows, send, recv, sibling)

    def owners_took(src, dst, send, recv):
        sent_or_told(4, lambda count: many(src, count, send, recv).wait_send())

    def line_sum(src, dst, send, recv):
        many(dst, 7, send, recv).wait_recv()
        dst[zl] = src[seat]
        return jnp.sum(dst[...].astype(F32), axis=0)

    def share_columns(h, step, after):
        buf, send, recv = vec.at[h, step], ag_s.at[h, step], ag_r.at[h, step]
        pair_send, pair_recv = sib_s.at[h, step], sib_r.at[h, step]
        mine = buf.at[o]

        @pl.when(owning)
        def _():
            def go(z):
                copy_to(mine, mine, send, recv.at[seat], line(z)).start()

            farthest_first(5, 0, 8, go)
            copy_to(mine, mine, pair_send, pair_recv, sibling).start()
            after()

        yield

        def relay(k, z):
            piece = buf.at[c * 4 + k]
            copy_to(piece, piece, send, recv.at[k], line(z)).wait_recv()
            copy_to(piece, piece, pair_send, pair_recv, sibling).start()

        others(4, FIRST, relay)
        yield

        many(buf, 4, pair_send, pair_recv).wait()
        pl.when(owning)(lambda: many(buf, 7, send, recv.at[0]).wait_send())

    def tell_owners(src, dst, send, recv):
        def go(q):
            p = owner_at(q)

            @pl.when(p != me)
            def _():
                copy_to(src(q), dst.at[me], send, recv, any_dp(p)).start()

        loop(8, go)

    def owners_told(src, dst, send, recv):
        sent_or_told(8, lambda count: many(dst, count, send, recv).wait_send())
        pl.when(owning)(lambda: many(dst, 15, send, recv).wait_recv())

    def peers():
        x, y = lax.div(xy, 4), lax.rem(xy, 4)
        return [lax.rem(x + a, 4) * 4 + lax.rem(y + b, 4) for a, b in FAR_FIRST]

    def broadcast(src, dst, own, send, recv, where):
        for p in peers():
            copy_to(src, dst.at[own], send, recv, where(p)).start()

    def scatter(src, dst, own, send, recv, where):
        for p in peers():
            copy_to(src.at[p], dst.at[own], send, recv, where(p)).start()

    def gathered(dst, own, send, recv, where):
        many(dst, 15, send, recv).wait()

    def center_start(h, step, *columns):
        snr[h, step, xy] = to_row(*columns)
        broadcast(snr.at[h, step, xy], snr.at[h, step], xy, sn_s.at[h, step], sn_r.at[h, step], plane)

    def center_cross(h, step):
        return copy_to(scn.at[h, step, 0], scn.at[h, step, 1], sc_s.at[h, step], sc_r.at[h, step], across)

    def center_middle(h, step):
        gathered(snr.at[h, step], xy, sn_s.at[h, step], sn_r.at[h, step], plane)
        scn[h, step, 0] = jnp.sum(snr[h, step].reshape(16, 128), axis=0, keepdims=True)
        center_cross(h, step).start()

    def center_end(h, step):
        center_cross(h, step).wait()
        return scn[h, step, 0] + scn[h, step, 1]

    def predict(h, step, in_plane, in_cross):
        def tile(k):
            cols = rows_at(k, 256)
            values = vec[h, step].reshape(128, 512)
            ps[h, step, :, :, cols] = nn(values, flip[:, cols]).astype(BF16).reshape(16, 8, 256)

        loop(4, tile)
        out, back, send, recv = ps.at[h, step], pr.at[h, step], xs_s.at[h, step], xs_r.at[h, step]
        scatter(out, back, xy, send, recv, plane)
        in_plane()
        yield
        gathered(back, xy, send, recv, plane)

        pr[h, step, xy] = ps[h, step, xy]
        hs[h, step] = jnp.sum(pr[h, step].astype(F32), axis=0).astype(BF16)
        cross = copy_to(hs.at[h, step], hr.at[h, step], cr_s.at[h, step], cr_r.at[h, step], across)
        cross.start()
        in_cross()
        yield
        cross.wait()
        ph[h, step, xy] = (hs[h, step].astype(F32) + hr[h, step].astype(F32)).astype(BF16)
        whole, send, recv = ph.at[h, step], xg_s.at[h, step], xg_r.at[h, step]
        broadcast(whole.at[xy], whole, xy, send, recv, plane)
        yield
        gathered(whole, xy, send, recv, plane)

    weights = lambda q: wr.at[me], wr, w_s, w_r
    waiting = [lambda: owners_told(*weights)]

    def keep(h, slot, value):
        held[h, slot] = jnp.broadcast_to(value, (16, 128))

    def kept(h, slot):
        return held[h, slot][:, :1]

    def image_of(h, step, use):
        project(h, lambda: ph[h, step].reshape(128, 1024))
        block = ph[h, step].astype(F32).reshape(8, 16, 1024)
        middle = jnp.sum(block, axis=2, keepdims=True) * (1.0 / block.shape[2])
        sts[h, step] = to_rows(jnp.sum(block * block, axis=2, keepdims=True), middle)
        part[h] = part[h] - middle * wr[me][None]
        pair_up(h, 1 + step).start()
        told = str_.at[h, step]
        stats = lambda q: sts.at[h, step, q], told, st_s.at[h, step], st_r.at[h, step]
        tell_owners(*stats)
        yield
        rems[h, step] = pairs(h, 1 + step).astype(BF16)
        moved = rems.at[h, step], remr.at[h, step], rem_s.at[h, step], rem_r.at[h, step]
        to_owners(*moved)
        yield
        while waiting:
            waiting.pop()()
        owners_told(*stats)

        @pl.when(owning)
        def _():
            told[me] = sts[h, step, o]
            rows = told[...]
            squares = from_row(jnp.sum(rows, axis=0), 0)
            lifted = jnp.sum(from_rows(rows, 1) * wr[...], axis=0)
            use((line_sum(*moved) + lifted) * (1.0 / n_total), squares * (1.0 / n_total))

        owners_took(*moved)

    def chain(h):
        project(h, lambda: tt[h])
        yield
        pair_up(h, 0).start()
        yield
        both = pairs(h, 0)
        high = both.astype(BF16)
        his[h] = high
        los[h] = (both - high.astype(F32)).astype(BF16)
        highs = his.at[h], hir.at[h], hi_s.at[h], hi_r.at[h]
        lows = los.at[h], lor.at[h], lo_s.at[h], lo_r.at[h]
        to_owners(*highs)
        yield

        @pl.when(owning)
        def _():
            bacc[h] = line_sum(*highs)
            vec[h, 0, o] = (bacc[h] * unscale).astype(BF16)

        yield from share_columns(h, 0, lambda: None)
        owners_took(*highs)

        def finish_right_side():
            @pl.when(owning)
            def _():
                bacc[h] = (bacc[h] + line_sum(*lows)) * unscale
                center_start(h, 0, total(bacc[h] * bacc[h]))

            owners_took(*lows)

        yield from predict(h, 0, lambda: to_owners(*lows), finish_right_side)

        def open_first(summed, squares):
            norm = from_row(center_end(h, 0), 0)
            image = summed + 0.5 * bacc[h]
            guess = norm / (squares + 0.5 * norm + EPS)
            near = bacc[h] - guess * image
            dacc[h] = image
            keep(h, 0, norm)
            keep(h, 1, guess)
            center_start(h, 1, total(bacc[h] * image), total(near * near), total(near * image), total(image * image))

        pl.when(owning)(lambda: center_middle(h, 0))
        yield from image_of(h, 0, open_first)
        yield
        pl.when(owning)(lambda: center_middle(h, 1))
        yield

        @pl.when(owning)
        def _():
            sums = center_end(h, 1)
            norm, guess = kept(h, 0), kept(h, 1)
            step_0 = norm / (from_row(sums, 0) + EPS)
            off = step_0 - guess
            norm_1 = from_row(sums, 1) - 2.0 * off * from_row(sums, 2) + off * off * from_row(sums, 3)
            racc[h] = bacc[h] - step_0 * dacc[h]
            dacc[h] = racc[h] + norm_1 / (norm + EPS) * bacc[h]
            vec[h, 1, o] = dacc[h].astype(BF16)
            keep(h, 2, step_0)
            keep(h, 3, norm_1)

        yield from share_columns(h, 1, lambda: center_start(h, 2, total(dacc[h] * dacc[h])))
        yield from predict(h, 1, lambda: pl.when(owning)(lambda: center_middle(h, 2)), lambda: None)
        send_all, recv_all = fin_s.at[h], fin_r.at[h]

        def close(summed, squares):
            image = summed + 0.5 * dacc[h]
            step_1 = kept(h, 3) / (squares + 0.5 * from_row(center_end(h, 2), 0) + EPS)
            vec[h, 2, o] = (racc[h] - step_1 * image).astype(BF16)
            finr[h, o] = to_row(kept(h, 2), step_1)

        def announce():
            def go(k):
                p = lax.rem(me + k + 1, 16)
                copy_to(finr.at[h, o], finr.at[h, o], send_all, recv_all, any_dp(p)).start()

            loop(15, go)

        yield from image_of(h, 1, close)
        yield from share_columns(h, 2, announce)

        sent_or_told(8, lambda count: many(finr.at[h], count, send_all, recv_all).wait_recv())
        pl.when(owning)(lambda: many(snr.at[h, 0], 15, send_all, recv_all).wait_send())

        first, second = from_rows(finr[h], 0), from_rows(finr[h], 1)
        part[h] = first * vec[h, 0].astype(F32) + second * vec[h, 1].astype(F32)

        def turn(k):
            rows = rows_at(k, 128)
            cols = pl.ds(h * 128, 128)
            coef_ref[rows, cols] = jnp.transpose(part[h, :, :, rows].reshape(128, 128))
            res_ref[rows, cols] = jnp.transpose(vec[h, 2, :, :, rows].astype(F32).reshape(128, 128))

        loop(4, turn)

    chains = [chain(0), chain(1)]
    for half in chains:
        next(half)
    pl.semaphore_wait(barrier, 31)
    turns = 0
    while chains:
        for half in list(chains):
            if next(half, "done") == "done":
                chains.remove(half)
        turns += 1
        if turns == 2:
            prepare()


def on_device(features, centers, targets):
    n_total = features.shape[0] * lax.axis_size("dp")
    vmem, dma = pltpu.VMEM, pltpu.SemaphoreType.DMA
    whole = pl.BlockSpec(memory_space=pltpu.VMEM)
    out = jax.ShapeDtypeStruct((centers.shape[0], targets.shape[1]), F32)
    buffers = [
        vmem((1024, 1024), BF16), vmem((512, 1024), BF16), vmem((1024, 256), BF16),
        vmem((1024, 512), BF16), vmem((512, 1024), BF16), vmem((2, 128, 1024), BF16), vmem((2, 8, 16, 512), F32),
        vmem((2, 3, 4, 16, 512), F32), vmem((2, 4, 16, 512), BF16), vmem((2, 8, 16, 512), BF16),
        vmem((2, 4, 16, 512), BF16), vmem((2, 8, 16, 512), BF16), vmem((2, 3, 8, 16, 512), BF16),
        vmem((2, 2, 16, 8, 1024), BF16), vmem((2, 2, 16, 8, 1024), BF16),
        vmem((2, 2, 8, 1024), BF16), vmem((2, 2, 8, 1024), BF16), vmem((2, 2, 16, 8, 1024), BF16),
        vmem((2, 2, 8, 1, 128), F32), vmem((2, 2, 16, 1, 128), F32), vmem((16, 1, 512), F32),
        vmem((2, 2, 4, 16, 512), BF16), vmem((2, 2, 8, 16, 512), BF16),
        vmem((2, 3, 16, 1, 128), F32), vmem((2, 3, 2, 1, 128), F32), vmem((2, 8, 1, 128), F32),
        vmem((2, 16, 512), F32), vmem((2, 16, 512), F32), vmem((2, 16, 512), F32), vmem((2, 4, 16, 128), F32),
        dma((4,)), dma, dma,
    ]
    semaphores = []
    for send, recv in (
        ((2, 3), (2, 3)), ((2,), (2,)), ((2,), (2,)), ((2, 3), (2, 3, 4)), ((2, 3), (2, 3)),
        ((2, 2), (2, 2)), ((2, 2), (2, 2)), ((2, 2), (2, 2)), ((2, 2), (2, 2)), ((), ()),
        ((2, 2), (2, 2)), ((2, 3), (2, 3)), ((2, 3), (2, 3)), ((2,), (2,)),
    ):
        semaphores += [dma(send), dma(recv)]
    return pl.pallas_call(
        functools.partial(kernel, n_total),
        out_shape=(out, out),
        in_specs=[pl.BlockSpec(memory_space=pl.ANY)] * 3,
        out_specs=(whole, whole),
        scratch_shapes=buffers + semaphores,
        compiler_params=pltpu.CompilerParams(
            collective_id=0, has_side_effects=True, vmem_limit_bytes=60 * 1024 * 1024
        ),
    )(features, centers, targets)


def solution(mesh):
    placed = (P("dp", None), P("center", None), P("dp", None))
    return jax.shard_map(
        on_device,
        mesh=mesh,
        in_specs=placed,
        out_specs=(P("center", None), P("center", None)),
        check_vma=False,
    )
```

```python
import functools
import math

import jax
import jax.numpy as jnp
from jax import lax
from jax.experimental import pallas as pl
from jax.experimental.pallas import tpu as pltpu
from jax.sharding import PartitionSpec as P

MESH = pl.DeviceIdType.MESH
F32, BF16 = jnp.float32, jnp.bfloat16
EPS = 1e-06
FAR_FIRST = sorted(
    ((a, b) for a in range(4) for b in range(4) if a + b), key=lambda t: -min(t[0], 4 - t[0]) - min(t[1], 4 - t[1])
)
FIRST = 2


def nt(a, b):
    return lax.dot_general(a, b, (((1,), (1,)), ((), ())), preferred_element_type=F32)


def nn(a, b):
    return lax.dot_general(a, b, (((1,), (0,)), ((), ())), preferred_element_type=F32)


def total(x):
    return jnp.sum(x, axis=1, keepdims=True)


def diagonal(slot):
    lane = lax.broadcasted_iota(jnp.int32, (16, 128), 1)
    return lane == lax.broadcasted_iota(jnp.int32, (16, 128), 0) + 16 * slot


def to_row(*columns):
    held = jnp.zeros((16, 128), F32)
    for slot, column in enumerate(columns):
        held = jnp.where(diagonal(slot), column, held)
    return jnp.sum(held, axis=0, keepdims=True)


def from_row(row, slot):
    return total(jnp.where(diagonal(slot), jnp.broadcast_to(row, (16, 128)), 0.0))


def to_rows(*columns):
    held = jnp.zeros((8, 16, 128), F32)
    for slot, column in enumerate(columns):
        held = jnp.where(diagonal(slot)[None], column, held)
    return jnp.sum(held, axis=1, keepdims=True)


def from_rows(rows, slot):
    spread = jnp.where(diagonal(slot)[None], jnp.broadcast_to(rows, (rows.shape[0], 16, 128)), 0.0)
    return jnp.sum(spread, axis=2, keepdims=True)


def copy_to(src, dst, send, recv, where):
    return pltpu.make_async_remote_copy(
        src_ref=src, dst_ref=dst, send_sem=send, recv_sem=recv, device_id=where, device_id_type=MESH
    )


def loop(count, body):
    def step(k, carry):
        body(k)
        return carry

    lax.fori_loop(0, count, step, 0)


def kernel(
    n_total, f_hbm, c_hbm, t_hbm, coef_ref, res_ref,
    f_ref, c_ref, t_ref, kern, flip, tt, part, pair_in, his, hir, los, lor, vec,
    ps, pr, hs, hr, ph, sts, str_, wr, rems, remr, snr, scn, finr, bacc, dacc, racc, held,
    load_f, load_c, load_t,
    pair_s, pair_r, hi_s, hi_r, lo_s, lo_r, ag_s, ag_r, sib_s, sib_r,
    xs_s, xs_r, cr_s, cr_r, xg_s, xg_r, st_s, st_r, w_s, w_r, rem_s, rem_r, sn_s, sn_r, sc_s, sc_r, fin_s, fin_r,
):
    g, j = lax.axis_index("dp"), lax.axis_index("center")
    zl, c = lax.div(g, 2), lax.rem(g, 2)
    xy, zh = lax.div(j, 2), lax.rem(j, 2)
    me = c * 8 + zl
    owning = jnp.logical_and(zl >= FIRST, zl < FIRST + 4)
    seat = lax.clamp(0, zl - FIRST, 3)
    o = c * 4 + seat
    sibling = (zl * 2 + (1 - c), j)
    across = (g, xy * 2 + (1 - zh))

    def line(z):
        return (z * 2 + c, j)

    def any_dp(p):
        return (lax.rem(p, 8) * 2 + lax.div(p, 8), j)

    def owner_at(q):
        return lax.div(q, 4) * 8 + FIRST + lax.rem(q, 4)

    def plane(p):
        return (g, p * 2 + zh)

    barrier = pltpu.get_barrier_semaphore()

    def greet(where):
        pl.semaphore_signal(barrier, inc=1, device_id=where, device_id_type=MESH)

    greet(across)
    loop(15, lambda k: greet(any_dp(lax.rem(me + k + 1, 16))))
    loop(15, lambda k: greet(plane(lax.rem(xy + k + 1, 16))))

    scale = 0.5 / math.sqrt(f_ref.shape[1])
    unscale = 1.0 / math.sqrt(n_total)
    quarter = f_ref.shape[0] // 4

    def rows_at(k, size):
        return pl.ds(pl.multiple_of(k * size, size), size)

    def load(k):
        return pltpu.make_async_copy(f_hbm.at[rows_at(k, quarter)], f_ref.at[rows_at(k, quarter)], load_f.at[k])

    centers_in = pltpu.make_async_copy(c_hbm, c_ref, load_c)
    targets_in = pltpu.make_async_copy(t_hbm, t_ref, load_t)
    centers_in.start()
    loop(4, lambda k: load(k).start())
    targets_in.start()
    centers_in.wait()

    def kernel_rows(k):
        load(k).wait()
        rows = rows_at(k, quarter)

        def tile(i):
            cols = rows_at(i, 256)
            lifted = 1.0 + scale * nt(f_ref[rows, :], c_ref[cols, :])
            kern[rows, cols] = (lifted * lifted * lifted).astype(BF16)

        loop(2, tile)

    loop(4, kernel_rows)
    targets_in.wait()

    def turn_targets(k):
        at = rows_at(k, 256)
        turned = jnp.transpose(t_ref[at, :].astype(F32)).astype(BF16)
        tt[0, :, at] = turned[:128]
        tt[1, :, at] = turned[128:]

    loop(4, turn_targets)

    def weigh(k, held):
        return held + jnp.sum(kern[rows_at(k, 64), :].astype(F32), axis=0, keepdims=True)

    def prepare():
        def turn_kernel(k):
            rows = rows_at(k, 128)
            flip[:, rows] = jnp.transpose(kern[rows, :].astype(F32)).astype(BF16)

        loop(8, turn_kernel)
        wr[me] = lax.fori_loop(0, 16, weigh, jnp.zeros((1, 512), F32))
        tell_owners(*weights)

    def project(h, values):
        def tile(k):
            cols = rows_at(k, 256)
            part[h, :, :, cols] = nn(values(), kern[:, cols]).reshape(8, 16, 256)

        loop(2, tile)

    def pair_up(h, step):
        return copy_to(
            part.at[h, pl.ds((1 - c) * 4, 4)], pair_in.at[h, step], pair_s.at[h, step], pair_r.at[h, step], sibling
        )

    def pairs(h, step):
        pair_up(h, step).wait()
        return part[h, pl.ds(c * 4, 4)] + pair_in[h, step]

    def others(count, first, body):
        def visit(k):
            z = first + k

            @pl.when(z != zl)
            def _():
                body(k, z)

        loop(count, visit)

    def farthest_first(reach, low, high, body):
        def visit(k):
            for z in (zl + reach - k, zl - reach + k):

                @pl.when(jnp.logical_and(z >= low, z < high))
                def _():
                    body(z)

        loop(reach, visit)

    def to_owners(src, dst, send, recv):
        def go(z):
            k = z - FIRST
            copy_to(src.at[k], dst.at[zl], send, recv, line(z)).start()

        farthest_first(5, FIRST, FIRST + 4, go)

    def sent_or_told(count, wait):
        pl.when(owning)(lambda: wait(count - 1))
        pl.when(jnp.logical_not(owning))(lambda: wait(count))

    def many(ref, count, send, recv):
        rows = ref.at[pl.ds(0, count)]
        return copy_to(rows, rows, send, recv, sibling)

    def owners_took(src, dst, send, recv):
        sent_or_told(4, lambda count: many(src, count, send, recv).wait_send())

    def line_sum(src, dst, send, recv):
        many(dst, 7, send, recv).wait_recv()
        dst[zl] = src[seat]
        return jnp.sum(dst[...].astype(F32), axis=0)

    def share_columns(h, step, after, before=lambda: None, meanwhile=lambda: None):
        buf, send, recv = vec.at[h, step], ag_s.at[h, step], ag_r.at[h, step]
        pair_send, pair_recv = sib_s.at[h, step], sib_r.at[h, step]
        mine = buf.at[o]

        @pl.when(owning)
        def _():
            before()

            def go(z):
                copy_to(mine, mine, send, recv.at[seat], line(z)).start()

            farthest_first(5, 0, 8, go)
            copy_to(mine, mine, pair_send, pair_recv, sibling).start()
            after()

        yield
        meanwhile()

        def relay(k, z):
            piece = buf.at[c * 4 + k]
            copy_to(piece, piece, send, recv.at[k], line(z)).wait_recv()
            copy_to(piece, piece, pair_send, pair_recv, sibling).start()

        others(4, FIRST, relay)

        many(buf, 4, pair_send, pair_recv).wait()
        pl.when(owning)(lambda: many(buf, 7, send, recv.at[0]).wait_send())

    def tell_owners(src, dst, send, recv):
        def go(q):
            p = owner_at(q)

            @pl.when(p != me)
            def _():
                copy_to(src(q), dst.at[me], send, recv, any_dp(p)).start()

        loop(8, go)

    def owners_told(src, dst, send, recv):
        sent_or_told(8, lambda count: many(dst, count, send, recv).wait_send())
        pl.when(owning)(lambda: many(dst, 15, send, recv).wait_recv())

    def peers():
        x, y = lax.div(xy, 4), lax.rem(xy, 4)
        return [lax.rem(x + a, 4) * 4 + lax.rem(y + b, 4) for a, b in FAR_FIRST]

    def broadcast(src, dst, own, send, recv, where):
        for p in peers():
            copy_to(src, dst.at[own], send, recv, where(p)).start()

    def scatter(src, dst, own, send, recv, where):
        for p in peers():
            copy_to(src.at[p], dst.at[own], send, recv, where(p)).start()

    def gathered(dst, own, send, recv, where):
        many(dst, 15, send, recv).wait()

    def center_start(h, step, *columns):
        snr[h, step, xy] = to_row(*columns)
        broadcast(snr.at[h, step, xy], snr.at[h, step], xy, sn_s.at[h, step], sn_r.at[h, step], plane)

    def center_cross(h, step):
        return copy_to(scn.at[h, step, 0], scn.at[h, step, 1], sc_s.at[h, step], sc_r.at[h, step], across)

    def center_middle(h, step):
        gathered(snr.at[h, step], xy, sn_s.at[h, step], sn_r.at[h, step], plane)
        scn[h, step, 0] = jnp.sum(snr[h, step].reshape(16, 128), axis=0, keepdims=True)
        center_cross(h, step).start()

    def center_end(h, step):
        center_cross(h, step).wait()
        return scn[h, step, 0] + scn[h, step, 1]

    def predict(h, step, in_plane, in_cross):
        def tile(k):
            cols = rows_at(k, 256)
            values = vec[h, step].reshape(128, 512)
            ps[h, step, :, :, cols] = nn(values, flip[:, cols]).astype(BF16).reshape(16, 8, 256)

        loop(4, tile)
        out, back, send, recv = ps.at[h, step], pr.at[h, step], xs_s.at[h, step], xs_r.at[h, step]
        scatter(out, back, xy, send, recv, plane)
        in_plane()
        yield
        gathered(back, xy, send, recv, plane)

        pr[h, step, xy] = ps[h, step, xy]
        hs[h, step] = jnp.sum(pr[h, step].astype(F32), axis=0).astype(BF16)
        cross = copy_to(hs.at[h, step], hr.at[h, step], cr_s.at[h, step], cr_r.at[h, step], across)
        cross.start()
        in_cross()
        yield
        cross.wait()
        ph[h, step, xy] = (hs[h, step].astype(F32) + hr[h, step].astype(F32)).astype(BF16)
        whole, send, recv = ph.at[h, step], xg_s.at[h, step], xg_r.at[h, step]
        broadcast(whole.at[xy], whole, xy, send, recv, plane)
        yield
        gathered(whole, xy, send, recv, plane)

    weights = lambda q: wr.at[me], wr, w_s, w_r
    waiting = [lambda: owners_told(*weights)]

    def keep(h, slot, value):
        held[h, slot] = jnp.broadcast_to(value, (16, 128))

    def kept(h, slot):
        return held[h, slot][:, :1]

    def image_of(h, step, use):
        project(h, lambda: ph[h, step].reshape(128, 1024))
        block = ph[h, step].astype(F32).reshape(8, 16, 1024)
        middle = jnp.sum(block, axis=2, keepdims=True) * (1.0 / block.shape[2])
        sts[h, step] = to_rows(jnp.sum(block * block, axis=2, keepdims=True), middle)
        part[h] = part[h] - middle * wr[me][None]
        pair_up(h, 1 + step).start()
        told = str_.at[h, step]
        stats = lambda q: sts.at[h, step, q], told, st_s.at[h, step], st_r.at[h, step]
        tell_owners(*stats)
        rems[h, step] = pairs(h, 1 + step).astype(BF16)
        moved = rems.at[h, step], remr.at[h, step], rem_s.at[h, step], rem_r.at[h, step]
        to_owners(*moved)
        yield
        while waiting:
            waiting.pop()()
        owners_told(*stats)

        @pl.when(owning)
        def _():
            told[me] = sts[h, step, o]
            rows = told[...]
            squares = from_row(jnp.sum(rows, axis=0), 0)
            lifted = jnp.sum(from_rows(rows, 1) * wr[...], axis=0)
            use((line_sum(*moved) + lifted) * (1.0 / n_total), squares * (1.0 / n_total))

        owners_took(*moved)

    def chain(h):
        project(h, lambda: tt[h])
        yield
        pair_up(h, 0).start()
        both = pairs(h, 0)
        high = both.astype(BF16)
        his[h] = high
        los[h] = (both - high.astype(F32)).astype(BF16)
        highs = his.at[h], hir.at[h], hi_s.at[h], hi_r.at[h]
        lows = los.at[h], lor.at[h], lo_s.at[h], lo_r.at[h]
        to_owners(*highs)
        yield

        @pl.when(owning)
        def _():
            bacc[h] = line_sum(*highs)
            vec[h, 0, o] = (bacc[h] * unscale).astype(BF16)

        yield from share_columns(h, 0, lambda: None)
        owners_took(*highs)

        def finish_right_side():
            @pl.when(owning)
            def _():
                bacc[h] = (bacc[h] + line_sum(*lows)) * unscale
                center_start(h, 0, total(bacc[h] * bacc[h]))

            owners_took(*lows)

        yield from predict(h, 0, lambda: to_owners(*lows), finish_right_side)

        def open_first(summed, squares):
            norm = from_row(center_end(h, 0), 0)
            image = summed + 0.5 * bacc[h]
            guess = norm / (squares + 0.5 * norm + EPS)
            near = bacc[h] - guess * image
            dacc[h] = image
            keep(h, 0, norm)
            keep(h, 1, guess)
            center_start(h, 1, total(bacc[h] * image), total(near * near), total(near * image), total(image * image))

        pl.when(owning)(lambda: center_middle(h, 0))
        yield from image_of(h, 0, open_first)
        yield
        pl.when(owning)(lambda: center_middle(h, 1))
        yield

        @pl.when(owning)
        def _():
            sums = center_end(h, 1)
            norm, guess = kept(h, 0), kept(h, 1)
            step_0 = norm / (from_row(sums, 0) + EPS)
            off = step_0 - guess
            norm_1 = from_row(sums, 1) - 2.0 * off * from_row(sums, 2) + off * off * from_row(sums, 3)
            racc[h] = bacc[h] - step_0 * dacc[h]
            dacc[h] = racc[h] + norm_1 / (norm + EPS) * bacc[h]
            vec[h, 1, o] = dacc[h].astype(BF16)
            keep(h, 2, step_0)
            keep(h, 3, norm_1)

        yield from share_columns(h, 1, lambda: center_start(h, 2, total(dacc[h] * dacc[h])))
        yield from predict(h, 1, lambda: pl.when(owning)(lambda: center_middle(h, 2)), lambda: None)
        send_all, recv_all = fin_s.at[h], fin_r.at[h]

        def close(summed, squares):
            image = summed + 0.5 * dacc[h]
            step_1 = kept(h, 3) / (squares + 0.5 * from_row(center_end(h, 2), 0) + EPS)
            vec[h, 2, o] = (racc[h] - step_1 * image).astype(BF16)
            finr[h, o] = to_row(kept(h, 2), step_1)

        def announce():
            def go(k):
                p = lax.rem(me + k + 1, 16)
                copy_to(finr.at[h, o], finr.at[h, o], send_all, recv_all, any_dp(p)).start()

            loop(15, go)

        yield from image_of(h, 1, close)
        cols = pl.ds(h * 128, 128)

        def finish_coef():
            sent_or_told(8, lambda count: many(finr.at[h], count, send_all, recv_all).wait_recv())
            first, second = from_rows(finr[h], 0), from_rows(finr[h], 1)
            part[h] = first * vec[h, 0].astype(F32) + second * vec[h, 1].astype(F32)

            def turn(k):
                rows = rows_at(k, 128)
                coef_ref[rows, cols] = jnp.transpose(part[h, :, :, rows].reshape(128, 128))

            loop(4, turn)

        yield from share_columns(h, 2, lambda: None, announce, finish_coef)
        pl.when(owning)(lambda: many(snr.at[h, 0], 15, send_all, recv_all).wait_send())

        def turn_residual(k):
            rows = rows_at(k, 128)
            res_ref[rows, cols] = jnp.transpose(vec[h, 2, :, :, rows].astype(F32).reshape(128, 128))

        loop(4, turn_residual)

    chains = [chain(0), chain(1)]
    for half in chains:
        next(half)
    pl.semaphore_wait(barrier, 31)
    turns = 0
    while chains:
        for half in list(chains):
            if next(half, "done") == "done":
                chains.remove(half)
        turns += 1
        if turns == 2:
            prepare()


def on_device(features, centers, targets):
    n_total = features.shape[0] * lax.axis_size("dp")
    vmem, dma = pltpu.VMEM, pltpu.SemaphoreType.DMA
    whole = pl.BlockSpec(memory_space=pltpu.VMEM)
    out = jax.ShapeDtypeStruct((centers.shape[0], targets.shape[1]), F32)
    buffers = [
        vmem((1024, 1024), BF16), vmem((512, 1024), BF16), vmem((1024, 256), BF16),
        vmem((1024, 512), BF16), vmem((512, 1024), BF16), vmem((2, 128, 1024), BF16), vmem((2, 8, 16, 512), F32),
        vmem((2, 3, 4, 16, 512), F32), vmem((2, 4, 16, 512), BF16), vmem((2, 8, 16, 512), BF16),
        vmem((2, 4, 16, 512), BF16), vmem((2, 8, 16, 512), BF16), vmem((2, 3, 8, 16, 512), BF16),
        vmem((2, 2, 16, 8, 1024), BF16), vmem((2, 2, 16, 8, 1024), BF16),
        vmem((2, 2, 8, 1024), BF16), vmem((2, 2, 8, 1024), BF16), vmem((2, 2, 16, 8, 1024), BF16),
        vmem((2, 2, 8, 1, 128), F32), vmem((2, 2, 16, 1, 128), F32), vmem((16, 1, 512), F32),
        vmem((2, 2, 4, 16, 512), BF16), vmem((2, 2, 8, 16, 512), BF16),
        vmem((2, 3, 16, 1, 128), F32), vmem((2, 3, 2, 1, 128), F32), vmem((2, 8, 1, 128), F32),
        vmem((2, 16, 512), F32), vmem((2, 16, 512), F32), vmem((2, 16, 512), F32), vmem((2, 4, 16, 128), F32),
        dma((4,)), dma, dma,
    ]
    semaphores = []
    for send, recv in (
        ((2, 3), (2, 3)), ((2,), (2,)), ((2,), (2,)), ((2, 3), (2, 3, 4)), ((2, 3), (2, 3)),
        ((2, 2), (2, 2)), ((2, 2), (2, 2)), ((2, 2), (2, 2)), ((2, 2), (2, 2)), ((), ()),
        ((2, 2), (2, 2)), ((2, 3), (2, 3)), ((2, 3), (2, 3)), ((2,), (2,)),
    ):
        semaphores += [dma(send), dma(recv)]
    return pl.pallas_call(
        functools.partial(kernel, n_total),
        out_shape=(out, out),
        in_specs=[pl.BlockSpec(memory_space=pl.ANY)] * 3,
        out_specs=(whole, whole),
        scratch_shapes=buffers + semaphores,
        compiler_params=pltpu.CompilerParams(
            collective_id=0, has_side_effects=True, vmem_limit_bytes=60 * 1024 * 1024
        ),
    )(features, centers, targets)


def solution(mesh):
    placed = (P("dp", None), P("center", None), P("dp", None))
    return jax.shard_map(
        on_device,
        mesh=mesh,
        in_specs=placed,
        out_specs=(P("center", None), P("center", None)),
        check_vma=False,
    )
```

```python
import functools
import math

import jax
import jax.numpy as jnp
from jax import lax
from jax.experimental import pallas as pl
from jax.experimental.pallas import tpu as pltpu
from jax.sharding import PartitionSpec as P

MESH = pl.DeviceIdType.MESH
F32, BF16 = jnp.float32, jnp.bfloat16
EPS = 1e-06
FAR_FIRST = sorted(
    ((a, b) for a in range(4) for b in range(4) if a + b), key=lambda t: -min(t[0], 4 - t[0]) - min(t[1], 4 - t[1])
)
FIRST = 2


def nt(a, b):
    return lax.dot_general(a, b, (((1,), (1,)), ((), ())), preferred_element_type=F32)


def nn(a, b):
    return lax.dot_general(a, b, (((1,), (0,)), ((), ())), preferred_element_type=F32)


def total(x):
    return jnp.sum(x, axis=1, keepdims=True)


def diagonal(slot):
    lane = lax.broadcasted_iota(jnp.int32, (16, 128), 1)
    return lane == lax.broadcasted_iota(jnp.int32, (16, 128), 0) + 16 * slot


def to_row(*columns):
    held = jnp.zeros((16, 128), F32)
    for slot, column in enumerate(columns):
        held = jnp.where(diagonal(slot), column, held)
    return jnp.sum(held, axis=0, keepdims=True)


def from_row(row, slot):
    return total(jnp.where(diagonal(slot), jnp.broadcast_to(row, (16, 128)), 0.0))


def to_rows(*columns):
    held = jnp.zeros((8, 16, 128), F32)
    for slot, column in enumerate(columns):
        held = jnp.where(diagonal(slot)[None], column, held)
    return jnp.sum(held, axis=1, keepdims=True)


def from_rows(rows, slot):
    spread = jnp.where(diagonal(slot)[None], jnp.broadcast_to(rows, (rows.shape[0], 16, 128)), 0.0)
    return jnp.sum(spread, axis=2, keepdims=True)


def copy_to(src, dst, send, recv, where):
    return pltpu.make_async_remote_copy(
        src_ref=src, dst_ref=dst, send_sem=send, recv_sem=recv, device_id=where, device_id_type=MESH
    )


def loop(count, body):
    def step(k, carry):
        body(k)
        return carry

    lax.fori_loop(0, count, step, 0, unroll=count < 6)


def kernel(
    n_total, f_hbm, c_hbm, t_hbm, coef_ref, res_ref,
    f_ref, c_ref, t_ref, kern, flip, tt, part, pair_in, his, hir, los, lor, vec,
    ps, pr, hs, hr, ph, sts, str_, wr, rems, remr, snr, scn, finr, bacc, dacc, racc, held,
    load_f, load_c, load_t,
    pair_s, pair_r, hi_s, hi_r, lo_s, lo_r, ag_s, ag_r, sib_s, sib_r,
    xs_s, xs_r, cr_s, cr_r, xg_s, xg_r, st_s, st_r, w_s, w_r, rem_s, rem_r, sn_s, sn_r, sc_s, sc_r, fin_s, fin_r,
):
    g, j = lax.axis_index("dp"), lax.axis_index("center")
    zl, c = lax.div(g, 2), lax.rem(g, 2)
    xy, zh = lax.div(j, 2), lax.rem(j, 2)
    me = c * 8 + zl
    owning = jnp.logical_and(zl >= FIRST, zl < FIRST + 4)
    seat = lax.clamp(0, zl - FIRST, 3)
    o = c * 4 + seat
    sibling = (zl * 2 + (1 - c), j)
    across = (g, xy * 2 + (1 - zh))

    def line(z):
        return (z * 2 + c, j)

    def any_dp(p):
        return (lax.rem(p, 8) * 2 + lax.div(p, 8), j)

    def owner_at(q):
        return lax.div(q, 4) * 8 + FIRST + lax.rem(q, 4)

    def plane(p):
        return (g, p * 2 + zh)

    barrier = pltpu.get_barrier_semaphore()

    def greet(where):
        pl.semaphore_signal(barrier, inc=1, device_id=where, device_id_type=MESH)

    greet(across)
    loop(15, lambda k: greet(any_dp(lax.rem(me + k + 1, 16))))
    loop(15, lambda k: greet(plane(lax.rem(xy + k + 1, 16))))

    scale = 0.5 / math.sqrt(f_ref.shape[1])
    unscale = 1.0 / math.sqrt(n_total)
    quarter = f_ref.shape[0] // 4

    def rows_at(k, size):
        return pl.ds(pl.multiple_of(k * size, size), size)

    def load(k):
        return pltpu.make_async_copy(f_hbm.at[rows_at(k, quarter)], f_ref.at[rows_at(k, quarter)], load_f.at[k])

    centers_in = pltpu.make_async_copy(c_hbm, c_ref, load_c)
    targets_in = pltpu.make_async_copy(t_hbm, t_ref, load_t)
    centers_in.start()
    loop(4, lambda k: load(k).start())
    targets_in.start()
    centers_in.wait()

    def kernel_rows(k):
        load(k).wait()
        rows = rows_at(k, quarter)

        def tile(i):
            cols = rows_at(i, 256)
            lifted = 1.0 + scale * nt(f_ref[rows, :], c_ref[cols, :])
            kern[rows, cols] = (lifted * lifted * lifted).astype(BF16)

        loop(2, tile)

    loop(4, kernel_rows)
    targets_in.wait()

    def turn_targets(k):
        at = rows_at(k, 256)
        turned = jnp.transpose(t_ref[at, :].astype(F32)).astype(BF16)
        tt[0, :, at] = turned[:128]
        tt[1, :, at] = turned[128:]

    loop(4, turn_targets)

    def weigh(k, held):
        return held + jnp.sum(kern[rows_at(k, 64), :].astype(F32), axis=0, keepdims=True)

    def prepare():
        def turn_kernel(k):
            rows = rows_at(k, 128)
            flip[:, rows] = jnp.transpose(kern[rows, :].astype(F32)).astype(BF16)

        loop(8, turn_kernel)
        wr[me] = lax.fori_loop(0, 16, weigh, jnp.zeros((1, 512), F32))
        tell_owners(*weights)

    def project(h, values):
        def tile(k):
            cols = rows_at(k, 256)
            part[h, :, :, cols] = nn(values(), kern[:, cols]).reshape(8, 16, 256)

        loop(2, tile)

    def pair_up(h, step):
        return copy_to(
            part.at[h, pl.ds((1 - c) * 4, 4)], pair_in.at[h, step], pair_s.at[h, step], pair_r.at[h, step], sibling
        )

    def pairs(h, step):
        pair_up(h, step).wait()
        return part[h, pl.ds(c * 4, 4)] + pair_in[h, step]

    def others(count, first, body):
        def visit(k):
            z = first + k

            @pl.when(z != zl)
            def _():
                body(k, z)

        loop(count, visit)

    def farthest_first(reach, low, high, body):
        def visit(k):
            for z in (zl + reach - k, zl - reach + k):

                @pl.when(jnp.logical_and(z >= low, z < high))
                def _():
                    body(z)

        loop(reach, visit)

    def to_owners(src, dst, send, recv):
        def go(z):
            k = z - FIRST
            copy_to(src.at[k], dst.at[zl], send, recv, line(z)).start()

        farthest_first(5, FIRST, FIRST + 4, go)

    def sent_or_told(count, wait):
        pl.when(owning)(lambda: wait(count - 1))
        pl.when(jnp.logical_not(owning))(lambda: wait(count))

    def many(ref, count, send, recv):
        rows = ref.at[pl.ds(0, count)]
        return copy_to(rows, rows, send, recv, sibling)

    def owners_took(src, dst, send, recv):
        sent_or_told(4, lambda count: many(src, count, send, recv).wait_send())

    def line_sum(src, dst, send, recv):
        many(dst, 7, send, recv).wait_recv()
        dst[zl] = src[seat]
        return jnp.sum(dst[...].astype(F32), axis=0)

    def share_columns(h, step, after, before=lambda: None, meanwhile=lambda: None):
        buf, send, recv = vec.at[h, step], ag_s.at[h, step], ag_r.at[h, step]
        pair_send, pair_recv = sib_s.at[h, step], sib_r.at[h, step]
        mine = buf.at[o]

        @pl.when(owning)
        def _():
            before()

            def go(z):
                copy_to(mine, mine, send, recv.at[seat], line(z)).start()

            farthest_first(5, 0, 8, go)
            copy_to(mine, mine, pair_send, pair_recv, sibling).start()
            after()

        yield
        meanwhile()

        def relay(k, z):
            piece = buf.at[c * 4 + k]
            copy_to(piece, piece, send, recv.at[k], line(z)).wait_recv()
            copy_to(piece, piece, pair_send, pair_recv, sibling).start()

        others(4, FIRST, relay)

        many(buf, 4, pair_send, pair_recv).wait()
        pl.when(owning)(lambda: many(buf, 7, send, recv.at[0]).wait_send())

    def tell_owners(src, dst, send, recv):
        def go(q):
            p = owner_at(q)

            @pl.when(p != me)
            def _():
                copy_to(src(q), dst.at[me], send, recv, any_dp(p)).start()

        loop(8, go)

    def owners_told(src, dst, send, recv):
        sent_or_told(8, lambda count: many(dst, count, send, recv).wait_send())
        pl.when(owning)(lambda: many(dst, 15, send, recv).wait_recv())

    def peers():
        x, y = lax.div(xy, 4), lax.rem(xy, 4)
        return [lax.rem(x + a, 4) * 4 + lax.rem(y + b, 4) for a, b in FAR_FIRST]

    def broadcast(src, dst, own, send, recv, where):
        for p in peers():
            copy_to(src, dst.at[own], send, recv, where(p)).start()

    def scatter(src, dst, own, send, recv, where):
        for p in peers():
            copy_to(src.at[p], dst.at[own], send, recv, where(p)).start()

    def gathered(dst, own, send, recv, where):
        many(dst, 15, send, recv).wait()

    def center_start(h, step, *columns):
        snr[h, step, xy] = to_row(*columns)
        broadcast(snr.at[h, step, xy], snr.at[h, step], xy, sn_s.at[h, step], sn_r.at[h, step], plane)

    def center_cross(h, step):
        return copy_to(scn.at[h, step, 0], scn.at[h, step, 1], sc_s.at[h, step], sc_r.at[h, step], across)

    def center_middle(h, step):
        gathered(snr.at[h, step], xy, sn_s.at[h, step], sn_r.at[h, step], plane)
        scn[h, step, 0] = jnp.sum(snr[h, step].reshape(16, 128), axis=0, keepdims=True)
        center_cross(h, step).start()

    def center_end(h, step):
        center_cross(h, step).wait()
        return scn[h, step, 0] + scn[h, step, 1]

    def predict(h, step, in_plane, in_cross):
        def tile(k):
            cols = rows_at(k, 256)
            values = vec[h, step].reshape(128, 512)
            ps[h, step, :, :, cols] = nn(values, flip[:, cols]).astype(BF16).reshape(16, 8, 256)

        loop(4, tile)
        out, back, send, recv = ps.at[h, step], pr.at[h, step], xs_s.at[h, step], xs_r.at[h, step]
        scatter(out, back, xy, send, recv, plane)
        in_plane()
        yield
        gathered(back, xy, send, recv, plane)

        pr[h, step, xy] = ps[h, step, xy]
        hs[h, step] = jnp.sum(pr[h, step].astype(F32), axis=0).astype(BF16)
        cross = copy_to(hs.at[h, step], hr.at[h, step], cr_s.at[h, step], cr_r.at[h, step], across)
        cross.start()
        in_cross()
        yield
        cross.wait()
        ph[h, step, xy] = (hs[h, step].astype(F32) + hr[h, step].astype(F32)).astype(BF16)
        whole, send, recv = ph.at[h, step], xg_s.at[h, step], xg_r.at[h, step]
        broadcast(whole.at[xy], whole, xy, send, recv, plane)
        yield
        gathered(whole, xy, send, recv, plane)

    weights = lambda q: wr.at[me], wr, w_s, w_r
    waiting = [lambda: owners_told(*weights)]

    def keep(h, slot, value):
        held[h, slot] = jnp.broadcast_to(value, (16, 128))

    def kept(h, slot):
        return held[h, slot][:, :1]

    def image_of(h, step, use):
        project(h, lambda: ph[h, step].reshape(128, 1024))
        block = ph[h, step].astype(F32).reshape(8, 16, 1024)
        middle = jnp.sum(block, axis=2, keepdims=True) * (1.0 / block.shape[2])
        sts[h, step] = to_rows(jnp.sum(block * block, axis=2, keepdims=True), middle)
        part[h] = part[h] - middle * wr[me][None]
        pair_up(h, 1 + step).start()
        told = str_.at[h, step]
        stats = lambda q: sts.at[h, step, q], told, st_s.at[h, step], st_r.at[h, step]
        tell_owners(*stats)
        rems[h, step] = pairs(h, 1 + step).astype(BF16)
        moved = rems.at[h, step], remr.at[h, step], rem_s.at[h, step], rem_r.at[h, step]
        to_owners(*moved)
        yield
        while waiting:
            waiting.pop()()
        owners_told(*stats)

        @pl.when(owning)
        def _():
            told[me] = sts[h, step, o]
            rows = told[...]
            squares = from_row(jnp.sum(rows, axis=0), 0)
            lifted = jnp.sum(from_rows(rows, 1) * wr[...], axis=0)
            use((line_sum(*moved) + lifted) * (1.0 / n_total), squares * (1.0 / n_total))

        owners_took(*moved)

    def chain(h):
        project(h, lambda: tt[h])
        yield
        pair_up(h, 0).start()
        both = pairs(h, 0)
        high = both.astype(BF16)
        his[h] = high
        los[h] = (both - high.astype(F32)).astype(BF16)
        highs = his.at[h], hir.at[h], hi_s.at[h], hi_r.at[h]
        lows = los.at[h], lor.at[h], lo_s.at[h], lo_r.at[h]
        to_owners(*highs)
        yield

        @pl.when(owning)
        def _():
            bacc[h] = line_sum(*highs)
            vec[h, 0, o] = (bacc[h] * unscale).astype(BF16)

        yield from share_columns(h, 0, lambda: None)
        owners_took(*highs)

        def finish_right_side():
            @pl.when(owning)
            def _():
                bacc[h] = (bacc[h] + line_sum(*lows)) * unscale
                center_start(h, 0, total(bacc[h] * bacc[h]))

            owners_took(*lows)

        yield from predict(h, 0, lambda: to_owners(*lows), finish_right_side)

        def open_first(summed, squares):
            norm = from_row(center_end(h, 0), 0)
            image = summed + 0.5 * bacc[h]
            guess = norm / (squares + 0.5 * norm + EPS)
            near = bacc[h] - guess * image
            dacc[h] = image
            keep(h, 0, norm)
            keep(h, 1, guess)
            center_start(h, 1, total(bacc[h] * image), total(near * near), total(near * image), total(image * image))

        pl.when(owning)(lambda: center_middle(h, 0))
        yield from image_of(h, 0, open_first)
        yield
        pl.when(owning)(lambda: center_middle(h, 1))
        yield

        @pl.when(owning)
        def _():
            sums = center_end(h, 1)
            norm, guess = kept(h, 0), kept(h, 1)
            step_0 = norm / (from_row(sums, 0) + EPS)
            off = step_0 - guess
            norm_1 = from_row(sums, 1) - 2.0 * off * from_row(sums, 2) + off * off * from_row(sums, 3)
            racc[h] = bacc[h] - step_0 * dacc[h]
            dacc[h] = racc[h] + norm_1 / (norm + EPS) * bacc[h]
            vec[h, 1, o] = dacc[h].astype(BF16)
            keep(h, 2, step_0)
            keep(h, 3, norm_1)

        yield from share_columns(h, 1, lambda: center_start(h, 2, total(dacc[h] * dacc[h])))
        yield from predict(h, 1, lambda: pl.when(owning)(lambda: center_middle(h, 2)), lambda: None)
        send_all, recv_all = fin_s.at[h], fin_r.at[h]

        def close(summed, squares):
            image = summed + 0.5 * dacc[h]
            step_1 = kept(h, 3) / (squares + 0.5 * from_row(center_end(h, 2), 0) + EPS)
            vec[h, 2, o] = (racc[h] - step_1 * image).astype(BF16)
            finr[h, o] = to_row(kept(h, 2), step_1)

        def announce():
            def go(k):
                p = lax.rem(me + k + 1, 16)
                copy_to(finr.at[h, o], finr.at[h, o], send_all, recv_all, any_dp(p)).start()

            loop(15, go)

        yield from image_of(h, 1, close)
        cols = pl.ds(h * 128, 128)

        def finish_coef():
            sent_or_told(8, lambda count: many(finr.at[h], count, send_all, recv_all).wait_recv())
            first, second = from_rows(finr[h], 0), from_rows(finr[h], 1)
            part[h] = first * vec[h, 0].astype(F32) + second * vec[h, 1].astype(F32)

            def turn(k):
                rows = rows_at(k, 128)
                coef_ref[rows, cols] = jnp.transpose(part[h, :, :, rows].reshape(128, 128))

            loop(4, turn)

        yield from share_columns(h, 2, lambda: None, announce, finish_coef)
        pl.when(owning)(lambda: many(snr.at[h, 0], 15, send_all, recv_all).wait_send())

        def turn_residual(k):
            rows = rows_at(k, 128)
            res_ref[rows, cols] = jnp.transpose(vec[h, 2, :, :, rows].astype(F32).reshape(128, 128))

        loop(4, turn_residual)

    chains = [chain(0), chain(1)]
    for half in chains:
        next(half)
    pl.semaphore_wait(barrier, 31)
    turns = 0
    while chains:
        for half in list(chains):
            if next(half, "done") == "done":
                chains.remove(half)
        turns += 1
        if turns == 2:
            prepare()


def on_device(features, centers, targets):
    n_total = features.shape[0] * lax.axis_size("dp")
    vmem, dma = pltpu.VMEM, pltpu.SemaphoreType.DMA
    whole = pl.BlockSpec(memory_space=pltpu.VMEM)
    out = jax.ShapeDtypeStruct((centers.shape[0], targets.shape[1]), F32)
    buffers = [
        vmem((1024, 1024), BF16), vmem((512, 1024), BF16), vmem((1024, 256), BF16),
        vmem((1024, 512), BF16), vmem((512, 1024), BF16), vmem((2, 128, 1024), BF16), vmem((2, 8, 16, 512), F32),
        vmem((2, 3, 4, 16, 512), F32), vmem((2, 4, 16, 512), BF16), vmem((2, 8, 16, 512), BF16),
        vmem((2, 4, 16, 512), BF16), vmem((2, 8, 16, 512), BF16), vmem((2, 3, 8, 16, 512), BF16),
        vmem((2, 2, 16, 8, 1024), BF16), vmem((2, 2, 16, 8, 1024), BF16),
        vmem((2, 2, 8, 1024), BF16), vmem((2, 2, 8, 1024), BF16), vmem((2, 2, 16, 8, 1024), BF16),
        vmem((2, 2, 8, 1, 128), F32), vmem((2, 2, 16, 1, 128), F32), vmem((16, 1, 512), F32),
        vmem((2, 2, 4, 16, 512), BF16), vmem((2, 2, 8, 16, 512), BF16),
        vmem((2, 3, 16, 1, 128), F32), vmem((2, 3, 2, 1, 128), F32), vmem((2, 8, 1, 128), F32),
        vmem((2, 16, 512), F32), vmem((2, 16, 512), F32), vmem((2, 16, 512), F32), vmem((2, 4, 16, 128), F32),
        dma((4,)), dma, dma,
    ]
    semaphores = []
    for send, recv in (
        ((2, 3), (2, 3)), ((2,), (2,)), ((2,), (2,)), ((2, 3), (2, 3, 4)), ((2, 3), (2, 3)),
        ((2, 2), (2, 2)), ((2, 2), (2, 2)), ((2, 2), (2, 2)), ((2, 2), (2, 2)), ((), ()),
        ((2, 2), (2, 2)), ((2, 3), (2, 3)), ((2, 3), (2, 3)), ((2,), (2,)),
    ):
        semaphores += [dma(send), dma(recv)]
    return pl.pallas_call(
        functools.partial(kernel, n_total),
        out_shape=(out, out),
        in_specs=[pl.BlockSpec(memory_space=pl.ANY)] * 3,
        out_specs=(whole, whole),
        scratch_shapes=buffers + semaphores,
        compiler_params=pltpu.CompilerParams(
            collective_id=0, has_side_effects=True, vmem_limit_bytes=60 * 1024 * 1024
        ),
    )(features, centers, targets)


def solution(mesh):
    placed = (P("dp", None), P("center", None), P("dp", None))
    return jax.shard_map(
        on_device,
        mesh=mesh,
        in_specs=placed,
        out_specs=(P("center", None), P("center", None)),
        check_vma=False,
    )
```
